128 devices in a mesh: tok: 32 (over y, z, core), head: 4 (over x).
Axes of the slice: x: 4, y: 4, z: 4, core: 2. Of those that a mesh axis runs over, the one named last changes fastest.
Arguments:
- queries: bfloat16 [32768, 4096], P(('tok', 'head')), may hold values from -64 to 64
- keys: bfloat16 [32768, 4096], P(('tok', 'head')), may hold values from -6 to 6
- values: bfloat16 [32768, 4096], P(('tok', 'head')), may hold values from -6 to 6
- token_rates: bfloat16 [32768, 8], P(('tok', 'head')), may hold values from 0.099609375 to 1
- gate_start: bfloat16 [8, 512, 1024], P('head'), may hold values from -0.25 to 0.25
- up_start: bfloat16 [8, 512, 1024], P('head'), may hold values from -0.25 to 0.25
- down_start: bfloat16 [8, 1024, 512], P('head'), may hold values from -0.1875 to 0.1875
- norm_gain: float32 [4096], replicated, may hold values from 0.25 to 1.75
- bounds: int32 [16], replicated, may hold values from 896 to 1152
Outputs:
- layer_out: bfloat16 [32768, 4096], P(('tok', 'head'))
The draws below stay inside these ranges and needn't reach their ends.
Inputs may be any that keep to these rules, and one draw needn't show every extreme that they name: The first span of segment s is its positions below bounds[s].
All inputs are finite; a program needn't handle non-finite values.
Results may differ from the reference program's by a relative error of at most 0.02.
Values may be sent and summed in bfloat16 or wider, within the bound.
No kernel may reach another device: no remote copies, remote signals or barrier semaphores. Data moves between devices by JAX's collectives and lax.ppermute only.
A program may use at most 192 MiB of HBM per device.

```python
import math
import jax
import jax.numpy as jnp
from jax import lax

FDIM = 512
HID = 1024
AHD = 128
WINDOW = 512
NS_ITERS = 3
FHEADS = 8
F = 4096
LEN = 2048
TOKENS = 32768
SEQS = 16
BOUND_LO = 896
BOUND_HI = 1152


def paired_fields(key):
    base_q = jnp.clip(jax.random.normal(jax.random.fold_in(key, 11), (TOKENS, F), jnp.float32), -6.0, 6.0)
    base_k = jnp.clip(jax.random.normal(jax.random.fold_in(key, 12), (TOKENS, F), jnp.float32), -6.0, 6.0)
    return (base_q, base_k)


def draw_queries(key, part):
    return paired_fields(key)[0].astype(jnp.bfloat16)


def draw_keys(key, part):
    return paired_fields(key)[1].astype(jnp.bfloat16)


def plant(drawn, own_key, low, top_value):
    longest = drawn.shape.index(max(drawn.shape))
    spots = []
    for shift in (0, 1):
        where = [jax.random.randint(jax.random.fold_in(own_key, axis), (), 0, length) for axis, length in enumerate(drawn.shape)]
        where[longest] = (where[longest] + shift) % drawn.shape[longest]
        spots.append(tuple(where))
    return drawn.at[spots[0]].set(low).at[spots[1]].set(top_value)


def steps_of(key, extent, pieces, least, high):
    def one(position, blocks):
        draws = jax.random.uniform(jax.random.fold_in(jax.random.fold_in(key, 6), position), (blocks,), jnp.float32, least / len(pieces), high / len(pieces))
        return jnp.repeat(jnp.exp(draws), extent[position] // blocks).reshape((-1,) + (1,) * (len(extent) - position - 1))

    level = one(*pieces[0])
    for cut in pieces[1:]:
        level = level * one(*cut)
    return level


def normal_values(own_key, shape, spread, most, split=(), kind=jnp.bfloat16):
    array = jax.random.normal(own_key, shape, jnp.float32) * spread
    if len(split) > 0:
        array = steps_of(own_key, shape, split, -0.22, 0.18) * array
    return jnp.clip(array, min=-most, max=most).astype(kind)


def setup_inputs(seed: int = 0) -> dict:
    seeds = jax.random.split(jax.random.key(seed), 10)
    return {
        "queries": draw_queries(jax.random.fold_in(seeds[9], 71), 0),
        "keys": draw_keys(jax.random.fold_in(seeds[9], 71), 0),
        "values": normal_values(seeds[2], (TOKENS, F), 1.0, 6.0, ((0, 128),)),
        "token_rates": jnp.clip(jnp.exp(math.log(1.0) - 2.306499 * jax.random.uniform(seeds[3], (TOKENS, FHEADS), jnp.float32) ** steps_of(seeds[3], (TOKENS, FHEADS), ((0, 128),), -0.2, 0.2)), 0.099609375, 1.0).astype(jnp.bfloat16),
        "gate_start": normal_values(seeds[4], (FHEADS, FDIM, HID), FDIM ** -0.5, 0.25, ((0, 4),)),
        "up_start": normal_values(seeds[5], (FHEADS, FDIM, HID), FDIM ** -0.5, 0.25, ((0, 4),)),
        "down_start": normal_values(seeds[6], (FHEADS, HID, FDIM), HID ** -0.5, 0.1875, ((0, 4),)),
        "norm_gain": jnp.clip(1.0 + 0.15 * jax.random.normal(seeds[7], (F,), jnp.float32), 0.25, 1.75),
        "bounds": plant(jax.random.randint(seeds[8], (SEQS,), BOUND_LO, BOUND_HI + 1), jax.random.fold_in(seeds[8], 1), BOUND_LO, BOUND_HI).astype(jnp.int32),
    }


linear_coef = 3.4445
cubic_coef = -4.775
quintic_coef = 2.0315
update_step = 1.0
rms_epsilon = 1e-05
norm_epsilon = 1e-06

def silu_slope(pre_act):
    logistic = jax.nn.sigmoid(pre_act)
    return logistic * (1.0 + pre_act * (1.0 - logistic))

def orthogonal(gradient):
    frob_norm = jnp.sqrt(jnp.sum(gradient * gradient) + norm_epsilon)
    iterate = (gradient / frob_norm).astype(jnp.bfloat16)
    for sweep_index in range(NS_ITERS):
        gram_matrix = jnp.dot(iterate, iterate.T, preferred_element_type=jnp.float32).astype(jnp.bfloat16)
        gram_square = jnp.dot(gram_matrix, gram_matrix, preferred_element_type=jnp.float32)
        poly_mix = (cubic_coef * gram_matrix.astype(jnp.float32) + quintic_coef * gram_square).astype(jnp.bfloat16)
        iterate = (linear_coef * iterate.astype(jnp.float32) + jnp.dot(poly_mix, iterate, preferred_element_type=jnp.float32)).astype(jnp.bfloat16)
    return iterate.astype(jnp.float32)

def renorm(updated, w_start):
    start_wide = w_start.astype(jnp.float32)
    target = jnp.sqrt(lax.optimization_barrier(jnp.sum(start_wide * start_wide, axis=0)) + norm_epsilon)
    actual = jnp.sqrt(lax.optimization_barrier(jnp.sum(updated * updated, axis=0)) + norm_epsilon)
    return (updated * (target / actual)).astype(jnp.bfloat16)

def swiglu_apply(in_rows, w_gate, w_up, w_down):
    pre_gate = jnp.dot(in_rows, w_gate, preferred_element_type=jnp.float32)
    pre_up = jnp.dot(in_rows, w_up, preferred_element_type=jnp.float32)
    hidden = (jax.nn.silu(pre_gate) * pre_up).astype(jnp.bfloat16)
    return jnp.dot(hidden, w_down, preferred_element_type=jnp.float32)

def fast_item(q_item, k_item, v_item, rate_row, span_bound, w_gate, w_up, w_down, gain_head):
    length = q_item.shape[0]
    split_low = length // 2 - length // 16
    split_high = length // 2 + length // 16
    in_span = jnp.arange(split_high) < span_bound
    k_rows = k_item[:split_high]
    pre_gate = jnp.dot(k_rows, w_gate, preferred_element_type=jnp.float32)
    pre_up = jnp.dot(k_rows, w_up, preferred_element_type=jnp.float32)
    active = jax.nn.silu(pre_gate)
    hidden = (active * pre_up).astype(jnp.bfloat16)
    weighted = rate_row[:split_high].astype(jnp.float32)[:, None] * v_item[:split_high].astype(jnp.float32)
    target = jnp.where(in_span[:, None], weighted, 0.0).astype(jnp.bfloat16)
    grad_down = jnp.dot(hidden.T, target, preferred_element_type=jnp.float32)
    back_grad = jnp.dot(target, w_down.T, preferred_element_type=jnp.float32)
    d_gate = (back_grad * pre_up * silu_slope(pre_gate)).astype(jnp.bfloat16)
    d_up = (back_grad * active).astype(jnp.bfloat16)
    grad_gate = jnp.dot(k_rows.T, d_gate, preferred_element_type=jnp.float32)
    grad_up = jnp.dot(k_rows.T, d_up, preferred_element_type=jnp.float32)
    new_gate = renorm(w_gate.astype(jnp.float32) + update_step * orthogonal(grad_gate), w_gate)
    new_up = renorm(w_up.astype(jnp.float32) + update_step * orthogonal(grad_up), w_up)
    new_down = renorm(w_down.astype(jnp.float32) + update_step * orthogonal(grad_down.T).T, w_down)
    before_out = swiglu_apply(q_item[:split_high], w_gate, w_up, w_down)
    after_out = swiglu_apply(q_item[split_low:], new_gate, new_up, new_down)
    middle = jnp.where((jnp.arange(split_low, split_high) < span_bound)[:, None], before_out[split_low:], after_out[:split_high - split_low])
    combined = jnp.concatenate([before_out[:split_low], middle, after_out[split_high - split_low:]], axis=0)
    root_mean = jnp.sqrt(lax.optimization_barrier(jnp.mean(combined * combined, axis=-1, keepdims=True)) + rms_epsilon)
    return (combined / root_mean * gain_head.astype(jnp.float32)).astype(jnp.bfloat16)

def attend_stream(queries, keys, values):
    block_len = min(LEN, 512)
    block_count = TOKENS // block_len
    head_count = F // AHD
    padding = jnp.zeros((WINDOW, F), keys.dtype)
    key_padded = jnp.concatenate([padding, keys], axis=0)
    value_padded = jnp.concatenate([padding, values], axis=0)

    def one_block(block_index):
        start = (block_index * block_len).astype(jnp.int32)
        q_rows = lax.dynamic_slice_in_dim(queries, start, block_len, 0)
        k_rows = lax.dynamic_slice_in_dim(key_padded, start, block_len + WINDOW, 0)
        v_rows = lax.dynamic_slice_in_dim(value_padded, start, block_len + WINDOW, 0)
        q_heads = q_rows.astype(jnp.float32).reshape(block_len, head_count, AHD)
        k_heads = k_rows.astype(jnp.float32).reshape(block_len + WINDOW, head_count, AHD)
        v_heads = v_rows.astype(jnp.float32).reshape(block_len + WINDOW, head_count, AHD)
        scores = jnp.einsum('qhd,khd->hqk', q_heads, k_heads) / math.sqrt(AHD)
        query_place = start + jnp.arange(block_len).astype(jnp.int32)
        key_place = start - WINDOW + jnp.arange(block_len + WINDOW).astype(jnp.int32)
        pos_gap = query_place[:, None] - key_place[None, :]
        allowed = ((pos_gap >= 0) & (pos_gap < WINDOW) & (key_place[None, :] >= 0))[None]
        masked = jnp.where(allowed, scores, -jnp.inf)
        row_max = lax.optimization_barrier(jnp.max(masked, axis=-1, keepdims=True))
        weights = jnp.where(allowed, jnp.exp(masked - row_max), 0.0)
        row_total = lax.optimization_barrier(jnp.sum(weights, axis=-1))
        mixed_out = jnp.einsum('hqk,khd->qhd', weights.astype(jnp.bfloat16).astype(jnp.float32), v_heads)
        return (mixed_out / row_total.T[:, :, None]).reshape(block_len, F).astype(jnp.bfloat16)
    return lax.map(one_block, jnp.arange(block_count).astype(jnp.int32)).reshape(TOKENS, F)

def reference(queries, keys, values, token_rates, gate_start, up_start, down_start, norm_gain, bounds):
    attn = attend_stream(queries, keys, values)

    def split_heads(block):
        return block.reshape(SEQS, LEN, FHEADS, FDIM).transpose(0, 2, 1, 3)
    rate_items = token_rates.reshape(SEQS, LEN, FHEADS).transpose(0, 2, 1)
    gain_items = norm_gain.reshape(FHEADS, FDIM)

    def per_sequence(seq_args):
        span_bound = seq_args[4]

        def per_head(head_args):
            return fast_item(head_args[0], head_args[1], head_args[2], head_args[3], span_bound, head_args[4], head_args[5], head_args[6], head_args[7])
        return lax.map(per_head, (seq_args[0], seq_args[1], seq_args[2], seq_args[3], gate_start, up_start, down_start, gain_items))
    fast_items = lax.map(per_sequence, (split_heads(queries), split_heads(keys), split_heads(values), rate_items, bounds))
    fast_rows = fast_items.transpose(0, 2, 1, 3).reshape(TOKENS, F)
    return (attn.astype(jnp.float32) + fast_rows.astype(jnp.float32)).astype(jnp.bfloat16)
```

```python
import functools
import math

import jax
import jax.numpy as jnp
from jax import lax
from jax.experimental import pallas as pl
from jax.experimental.pallas import tpu as pltpu
from jax.sharding import PartitionSpec as P

FDIM = 512
HID = 1024
AHD = 128
WINDOW = 512
NS_ITERS = 3
LEN = 2048
HALF = 128
LOW = 896
HIGH = 1152
SPLIT = 8
BLOCK = LEN // SPLIT

linear_coef = 3.4445
cubic_coef = -4.775
quintic_coef = 2.0315
rms_epsilon = 1e-05
norm_epsilon = 1e-06
MASKED = -1e30
EXP2_SCALE = math.log2(math.e) / math.sqrt(AHD)

AXES = ("tok", "head")
F32 = jnp.float32
BF16 = jnp.bfloat16


def place_of(block):
    return (block % 4) * 2 + block // 4


def dot(a, b):
    return lax.dot_general(a, b, (((1,), (0,)), ((), ())), preferred_element_type=F32)


def dot_nt(a, b):
    return lax.dot_general(a, b, (((1,), (1,)), ((), ())), preferred_element_type=F32)


def update_kernel(
    scalars,
    k_hbm,
    v_hbm,
    rates,
    gate_hbm,
    up_hbm,
    down_hbm,
    new_gate,
    new_up,
    new_down,
    kbuf,
    vbuf,
    wg,
    wu,
    wd,
    wdt,
    hid,
    dgate,
    dup,
    target,
    kt,
    tt,
    grads,
    xs,
    grams,
    sems,
):
    bound = scalars[0]
    parity = scalars[1]
    owned = scalars[3]
    copies = []

    def fetch(src, dst):
        copy = pltpu.make_async_copy(src, dst, sems.at[len(copies)])
        copy.start()
        copies.append(copy)

    fetch(gate_hbm.at[parity], wg)
    fetch(up_hbm.at[parity], wu)
    fetch(down_hbm.at[parity], wd)
    for block in range(5):
        rows = min(BLOCK, HIGH - block * BLOCK)
        src = pl.ds(place_of(block) * BLOCK, rows)
        dst = pl.ds(block * BLOCK, rows)
        fetch(k_hbm.at[src], kbuf.at[dst])
        fetch(v_hbm.at[src], vbuf.at[dst])
    for copy in copies:
        copy.wait()

    wdt[...] = wd[...].T
    lane = lax.broadcasted_iota(jnp.int32, (1, 8), 1)
    pick = (lane == owned).astype(F32)
    step = 384
    for part in range(HIGH // step):
        rows = pl.ds(part * step, step)
        rate = jnp.sum(rates[rows, :].astype(F32) * pick, axis=1, keepdims=True)
        place = part * step + lax.broadcasted_iota(jnp.int32, (step, 1), 0)
        weighted = rate * vbuf[rows, :].astype(F32)
        target[rows, :] = jnp.where(place < bound, weighted, 0.0).astype(BF16)
        k_rows = kbuf[rows, :]
        t_rows = target[rows, :]
        for tile in range(HID // 256):
            cols = pl.ds(tile * 256, 256)
            pre_gate = dot(k_rows, wg[:, cols])
            pre_up = dot(k_rows, wu[:, cols])
            back = dot(t_rows, wdt[:, cols])
            logistic = 1.0 / (1.0 + jnp.exp(-pre_gate))
            act = pre_gate * logistic
            slope = logistic * (1.0 + pre_gate * (1.0 - logistic))
            hid[rows, cols] = (act * pre_up).astype(BF16)
            dgate[rows, cols] = (back * pre_up * slope).astype(BF16)
            dup[rows, cols] = (back * act).astype(BF16)
    kt[...] = kbuf[...].T
    tt[...] = target[...].T

    for which, (left, right) in enumerate(((kt, dgate), (kt, dup), (tt, hid))):
        total = jnp.zeros((1, 256), F32)
        for tile in range(HID // 256):
            cols = pl.ds(tile * 256, 256)
            grad = dot(left[...], right[:, cols])
            grads[which, :, cols] = grad
            total += jnp.sum(grad * grad, axis=0, keepdims=True)
        inv = 1.0 / jnp.sqrt(jnp.sum(total, axis=1, keepdims=True) + norm_epsilon)
        for tile in range(HID // 256):
            cols = pl.ds(tile * 256, 256)
            xs[which, :, cols] = (grads[which, :, cols] * inv).astype(BF16)

    def iteration(_, carry):
        for which in range(3):
            for tile in range(2):
                rows = pl.ds(tile * 256, 256)
                grams[which, :, rows] = dot_nt(xs[which], xs[which, rows, :]).astype(BF16)
        for which in range(3):
            gram = grams[which]
            for tile in range(2):
                cols = pl.ds(tile * 256, 256)
                mixed = cubic_coef * grams[which, :, cols].astype(F32) + quintic_coef * dot(
                    gram, grams[which, :, cols]
                )
                grams[3 + which, :, cols] = mixed.astype(BF16)
        for which in range(3):
            mix = grams[3 + which]
            for tile in range(4):
                cols = pl.ds(tile * 256, 256)
                old = xs[which, :, cols]
                xs[which, :, cols] = (linear_coef * old.astype(F32) + dot(mix, old)).astype(BF16)
        return carry

    lax.fori_loop(0, NS_ITERS, iteration, 0)

    for which, (start, out) in enumerate(((wg, new_gate), (wu, new_up))):
        for tile in range(HID // 256):
            cols = pl.ds(tile * 256, 256)
            wide = start[:, cols].astype(F32)
            moved = wide + xs[which, :, cols].astype(F32)
            aim = jnp.sqrt(jnp.sum(wide * wide, axis=0, keepdims=True) + norm_epsilon)
            actual = jnp.sqrt(jnp.sum(moved * moved, axis=0, keepdims=True) + norm_epsilon)
            out[:, cols] = (moved * (aim / actual)).astype(BF16)
    for tile in range(FDIM // 128):
        rows = pl.ds(tile * 128, 128)
        wide = wdt[rows, :].astype(F32)
        moved = wide + xs[2, rows, :].astype(F32)
        aim = jnp.sqrt(jnp.sum(wide * wide, axis=1, keepdims=True) + norm_epsilon)
        actual = jnp.sqrt(jnp.sum(moved * moved, axis=1, keepdims=True) + norm_epsilon)
        new_down[:, rows] = (moved * (aim / actual)).astype(BF16).T


def fast_update(scalars, k_item, v_item, rates, gate_start, up_start, down_start):
    hbm = pl.BlockSpec(memory_space=pltpu.HBM)
    vmem = pl.BlockSpec(memory_space=pltpu.VMEM)
    return pl.pallas_call(
        update_kernel,
        name="fast_update",
        out_shape=(
            jax.ShapeDtypeStruct((FDIM, HID), BF16),
            jax.ShapeDtypeStruct((FDIM, HID), BF16),
            jax.ShapeDtypeStruct((HID, FDIM), BF16),
        ),
        in_specs=[pl.BlockSpec(memory_space=pltpu.SMEM), hbm, hbm, vmem, hbm, hbm, hbm],
        out_specs=(vmem, vmem, vmem),
        scratch_shapes=[
            pltpu.VMEM((HIGH, FDIM), BF16),
            pltpu.VMEM((HIGH, FDIM), BF16),
            pltpu.VMEM((FDIM, HID), BF16),
            pltpu.VMEM((FDIM, HID), BF16),
            pltpu.VMEM((HID, FDIM), BF16),
            pltpu.VMEM((FDIM, HID), BF16),
            pltpu.VMEM((HIGH, HID), BF16),
            pltpu.VMEM((HIGH, HID), BF16),
            pltpu.VMEM((HIGH, HID), BF16),
            pltpu.VMEM((HIGH, FDIM), BF16),
            pltpu.VMEM((FDIM, HIGH), BF16),
            pltpu.VMEM((FDIM, HIGH), BF16),
            pltpu.VMEM((3, FDIM, HID), F32),
            pltpu.VMEM((3, FDIM, HID), BF16),
            pltpu.VMEM((6, FDIM, FDIM), BF16),
            pltpu.SemaphoreType.DMA((13,)),
        ],
        compiler_params=pltpu.CompilerParams(vmem_limit_bytes=48 * 1024 * 1024),
        cost_estimate=pl.CostEstimate(
            flops=20_000_000_000, bytes_accessed=12_000_000, transcendentals=1_200_000
        ),
    )(scalars, k_item, v_item, rates, gate_start, up_start, down_start)


def apply_kernel(
    chunk,
    scalars,
    q_hbm,
    k_hbm,
    v_hbm,
    hk_hbm,
    hv_hbm,
    gate_hbm,
    up_hbm,
    down_hbm,
    new_gate,
    new_up,
    new_down,
    gain,
    out,
    qc,
    kbuf,
    vbuf,
    wg,
    wu,
    wd,
    hid,
    raw,
    before,
    fast,
    sems,
):
    bound = scalars[0]
    parity = scalars[1]
    sequence = scalars[2]
    owned = scalars[3]
    copies = []

    def fetch(src, dst):
        copy = pltpu.make_async_copy(src, dst, sems.at[len(copies)])
        copy.start()
        copies.append(copy)

    for block in range(SPLIT):
        src = pl.ds(place_of(block) * BLOCK + chunk * HALF, HALF)
        fetch(q_hbm.at[src], qc.at[pl.ds(block * HALF, HALF)])
    fetch(gate_hbm.at[parity], wg)
    fetch(up_hbm.at[parity], wu)
    fetch(down_hbm.at[parity], wd)
    first = len(copies)
    fetch(hk_hbm, kbuf.at[pl.ds(0, WINDOW)])
    fetch(hv_hbm, vbuf.at[pl.ds(0, WINDOW)])
    for block in range(SPLIT):
        src = pl.ds(place_of(block) * BLOCK, BLOCK)
        dst = pl.ds(WINDOW + block * BLOCK, BLOCK)
        fetch(k_hbm.at[src], kbuf.at[dst])
        fetch(v_hbm.at[src], vbuf.at[dst])
    for copy in copies[:first]:
        copy.wait()

    def swiglu(rows, gate, up, down, store):
        in_rows = qc[rows, :]
        for tile in range(HID // 256):
            cols = pl.ds(tile * 256, 256)
            pre_gate = dot(in_rows, gate[:, cols])
            pre_up = dot(in_rows, up[:, cols])
            hid[pl.ds(0, rows.size), cols] = (
                pre_gate / (1.0 + jnp.exp(-pre_gate)) * pre_up
            ).astype(BF16)
        store(dot(hid[pl.ds(0, rows.size), :], down[...]))

    edge = 4 if chunk == 0 else 3
    old_rows = pl.ds(0, (edge + 1) * HALF)
    new_rows = pl.ds(edge * HALF, (SPLIT - edge) * HALF)

    def store_old(value):
        raw[pl.ds(0, edge * HALF), :] = value[: edge * HALF]
        before[...] = value[edge * HALF :]

    def store_new(value):
        raw[new_rows, :] = value

    swiglu(old_rows, wg, wu, wd, store_old)
    swiglu(new_rows, new_gate, new_up, new_down, store_new)
    mid = pl.ds(edge * HALF, HALF)
    place = edge * BLOCK + chunk * HALF + lax.broadcasted_iota(jnp.int32, (HALF, 1), 0)
    raw[mid, :] = jnp.where(place < bound, before[...], raw[mid, :])
    gain_row = gain[pl.ds(owned, 1), :]
    for block in range(SPLIT):
        rows = pl.ds(block * HALF, HALF)
        value = raw[rows, :]
        root = jnp.sqrt(jnp.mean(value * value, axis=1, keepdims=True) + rms_epsilon)
        fast[rows, :] = (value / root * gain_row).astype(BF16)
    for copy in copies[first:]:
        copy.wait()

    row_iota = lax.broadcasted_iota(jnp.int32, (HALF, HALF), 0)
    col_iota = lax.broadcasted_iota(jnp.int32, (HALF, HALF), 1)
    keep_old = col_iota > row_iota
    keep_own = col_iota <= row_iota

    def attend(block, edge_block):
        base = pl.multiple_of(block * BLOCK + chunk * HALF, HALF)
        q_rows = pl.ds(pl.multiple_of(block * HALF, HALF), HALF)
        o_rows = pl.ds(pl.multiple_of(place_of(block) * HALF, HALF), HALF)
        keys = pl.ds(base, WINDOW + HALF)
        for head in range(FDIM // AHD):
            cols = pl.ds(head * AHD, AHD)
            scores = dot_nt(qc[q_rows, cols], kbuf[keys, cols])
            parts = [scores[:, i * HALF : (i + 1) * HALF] for i in range(5)]
            parts[0] = jnp.where(keep_old, parts[0], MASKED)
            parts[4] = jnp.where(keep_own, parts[4], MASKED)
            if edge_block:
                for i in range(4):
                    absent = (sequence == 0) & (base + i * HALF < WINDOW)
                    parts[i] = jnp.where(absent, MASKED, parts[i])
            masked = jnp.concatenate(parts, axis=1)
            top = jnp.max(masked, axis=1, keepdims=True)
            weights = jnp.exp2((masked - top) * EXP2_SCALE)
            total = jnp.sum(weights, axis=1, keepdims=True)
            mixed = dot(weights.astype(BF16), vbuf[keys, cols])
            attn = (mixed / total).astype(BF16)
            out[o_rows, cols] = (attn.astype(F32) + fast[q_rows, cols].astype(F32)).astype(BF16)

    def edge_body(block, carry):
        attend(block, True)
        return carry

    def main_body(block, carry):
        attend(block, False)
        return carry

    lax.fori_loop(0, 2, edge_body, 0)
    lax.fori_loop(2, SPLIT, main_body, 0)


def apply_chunk(
    chunk, scalars, q_item, k_item, v_item, halo_k, halo_v, starts, news, gain
):
    hbm = pl.BlockSpec(memory_space=pltpu.HBM)
    vmem = pl.BlockSpec(memory_space=pltpu.VMEM)
    rows = SPLIT * HALF
    return pl.pallas_call(
        functools.partial(apply_kernel, chunk),
        name="apply_attend",
        out_shape=jax.ShapeDtypeStruct((rows, FDIM), BF16),
        in_specs=[pl.BlockSpec(memory_space=pltpu.SMEM)] + [hbm] * 8 + [vmem] * 4,
        out_specs=vmem,
        scratch_shapes=[
            pltpu.VMEM((rows, FDIM), BF16),
            pltpu.VMEM((WINDOW + LEN, FDIM), BF16),
            pltpu.VMEM((WINDOW + LEN, FDIM), BF16),
            pltpu.VMEM((FDIM, HID), BF16),
            pltpu.VMEM((FDIM, HID), BF16),
            pltpu.VMEM((HID, FDIM), BF16),
            pltpu.VMEM((5 * HALF, HID), BF16),
            pltpu.VMEM((rows, FDIM), F32),
            pltpu.VMEM((HALF, FDIM), F32),
            pltpu.VMEM((rows, FDIM), BF16),
            pltpu.SemaphoreType.DMA((29,)),
        ],
        compiler_params=pltpu.CompilerParams(vmem_limit_bytes=40 * 1024 * 1024),
        cost_estimate=pl.CostEstimate(
            flops=8_000_000_000, bytes_accessed=14_000_000, transcendentals=4_000_000
        ),
    )(scalars, q_item, k_item, v_item, halo_k, halo_v, *starts, *news, gain)


def body(queries, keys, values, token_rates, gate_start, up_start, down_start, norm_gain, bounds):
    shards = lax.axis_size("tok") * lax.axis_size("head")
    column = lax.axis_index("head")
    parity = lax.axis_index("tok") % 2
    owned = 2 * column + parity
    sequence = lax.axis_index("tok") // 2
    groups = [
        [s * SPLIT + (i % 2) * 4 + i // 2 for i in range(SPLIT)] for s in range(shards // SPLIT)
    ]
    plain_groups = [[s * SPLIT + i for i in range(SPLIT)] for s in range(shards // SPLIT)]
    span_bound = lax.dynamic_index_in_dim(bounds, sequence, 0, keepdims=False)
    scalars = jnp.stack([span_bound, parity, sequence, owned]).astype(jnp.int32)

    def spread(array):
        return lax.all_to_all(
            array, AXES, split_axis=1, concat_axis=0, tiled=True, axis_index_groups=groups
        )

    def halo(item):
        tail = jnp.concatenate(
            [item[place_of(b) * BLOCK : (place_of(b) + 1) * BLOCK] for b in (6, 7)], axis=0
        )
        count = lax.axis_size("tok")
        return lax.ppermute(tail, "tok", [(i, i + 2) for i in range(count - 2)])

    rates = lax.all_gather(token_rates, AXES, axis=0, tiled=True, axis_index_groups=plain_groups)
    keys, rates = lax.optimization_barrier((keys, rates))
    k_item = spread(keys)
    v_item = spread(values)
    halo_k = halo(k_item)
    halo_v = halo(v_item)
    q_item = spread(queries)
    starts = (gate_start, up_start, down_start)
    news = fast_update(scalars, k_item, v_item, rates, *starts)
    gain = norm_gain.reshape(-1, FDIM)
    returned = []
    for chunk in range(2):
        out = apply_chunk(
            chunk, scalars, q_item, k_item, v_item, halo_k, halo_v, starts, news, gain
        )
        returned.append(
            lax.all_to_all(
                out, AXES, split_axis=0, concat_axis=1, tiled=True, axis_index_groups=groups
            )
        )
    return jnp.concatenate(returned, axis=0)


def solution(mesh):
    tokens = P(AXES, None)
    return jax.shard_map(
        body,
        mesh=mesh,
        in_specs=(
            tokens,
            tokens,
            tokens,
            tokens,
            P("head", None, None),
            P("head", None, None),
            P("head", None, None),
            P(),
            P(),
        ),
        out_specs=tokens,
        check_vma=False,
    )
```

```python
import functools
import math

import jax
import jax.numpy as jnp
from jax import lax
from jax.experimental import pallas as pl
from jax.experimental.pallas import tpu as pltpu
from jax.sharding import PartitionSpec as P

FDIM = 512
HID = 1024
AHD = 128
WINDOW = 512
NS_ITERS = 3
LEN = 2048
HALF = 128
LOW = 896
HIGH = 1152
SPLIT = 8
BLOCK = LEN // SPLIT

linear_coef = 3.4445
cubic_coef = -4.775
quintic_coef = 2.0315
rms_epsilon = 1e-05
norm_epsilon = 1e-06
MASKED = -1e30
EXP2_SCALE = math.log2(math.e) / math.sqrt(AHD)

AXES = ("tok", "head")
F32 = jnp.float32
BF16 = jnp.bfloat16


CHIPS = 4
KV_ROWS = 528
RATE_ROW = 512
VMEM_LIMIT = 60 * 1024 * 1024


def place_of(block):
    return (block % CHIPS) * 2 + block // CHIPS


class Fetcher:
    def __init__(self, sems):
        self.sems = sems
        self.copies = []

    def __call__(self, src, dst):
        copy = pltpu.make_async_copy(src, dst, self.sems.at[len(self.copies)])
        copy.start()
        self.copies.append(copy)

    def choose(self, options, dst):
        sem = self.sems.at[len(self.copies)]
        for cond, src in options:

            @pl.when(cond)
            def _(src=src):
                pltpu.make_async_copy(src, dst, sem).start()

        self.copies.append(pltpu.make_async_copy(options[0][1], dst, sem))

    def wait(self, first=0, last=None):
        for copy in self.copies[first:last]:
            copy.wait()


def position():
    column = lax.axis_index("head")
    tok = lax.axis_index("tok")
    return column, lax.rem(tok, 2), lax.div(tok, 2)


def pack_kv_kernel(keys, values, rates, *rest):
    outs = rest[: CHIPS + 1]
    kbuf, vbuf, lines, in_sems, sems = rest[CHIPS + 1 :]

    def out_at(index):
        return outs[index] if index < CHIPS else outs[CHIPS].at[index - CHIPS]

    column, parity, _ = position()
    load = Fetcher(in_sems)
    fetch = Fetcher(sems)
    load(keys, kbuf)
    load(values, vbuf)
    turned = rates[...].astype(F32)
    place = lax.broadcasted_iota(jnp.int32, turned.shape, 0)
    targets = []
    for which in range(2):
        core = parity if which == 0 else 1 - parity
        for slot in range(CHIPS):
            head = 2 * lax.rem(column + slot, CHIPS) + core
            targets.append((which * CHIPS + slot, head))
    for index, head in targets:
        line = jnp.sum(jnp.where(place == head, turned, 0.0), axis=0, keepdims=True)
        lines[index, :, pl.ds(0, BLOCK)] = jnp.broadcast_to(line, (16, BLOCK)).astype(BF16)
        lines[index, :, pl.ds(BLOCK, FDIM - BLOCK)] = jnp.zeros((16, FDIM - BLOCK), BF16)
    for index, head in targets:
        fetch(lines.at[index], out_at(index).at[pl.ds(RATE_ROW, 16)])
    for part, buf in ((0, kbuf), (1, vbuf)):
        load.wait(part, part + 1)
        for index, head in targets:
            cols = pl.ds(pl.multiple_of(head * FDIM, FDIM), FDIM)
            fetch(buf.at[:, cols], out_at(index).at[pl.ds(part * BLOCK, BLOCK)])
    fetch.wait()


def pack_kv(keys, values, rates):
    hbm = pl.BlockSpec(memory_space=pltpu.HBM)
    shape = jax.ShapeDtypeStruct((KV_ROWS, FDIM), BF16)
    outs = pl.pallas_call(
        pack_kv_kernel,
        name="pack_kv",
        out_shape=(shape,) * CHIPS + (jax.ShapeDtypeStruct((CHIPS, KV_ROWS, FDIM), BF16),),
        in_specs=[hbm, hbm, pl.BlockSpec(memory_space=pltpu.VMEM)],
        out_specs=(hbm,) * (CHIPS + 1),
        scratch_shapes=[
            pltpu.VMEM((BLOCK, CHIPS * 2 * FDIM), BF16),
            pltpu.VMEM((BLOCK, CHIPS * 2 * FDIM), BF16),
            pltpu.VMEM((2 * CHIPS, 16, FDIM), BF16),
            pltpu.SemaphoreType.DMA((2,)),
            pltpu.SemaphoreType.DMA((24,)),
        ],
        compiler_params=pltpu.CompilerParams(vmem_limit_bytes=VMEM_LIMIT),
        cost_estimate=pl.CostEstimate(flops=0, bytes_accessed=16_000_000, transcendentals=0),
    )(keys, values, rates)
    return outs[:CHIPS], outs[CHIPS]


def pack_q_kernel(queries, own, swap, qbuf, in_sems, sems):
    column, parity, _ = position()
    load = Fetcher(in_sems)
    fetch = Fetcher(sems)
    load(queries, qbuf)
    load.wait()
    for which in range(2):
        core = parity if which == 0 else 1 - parity
        for slot in range(CHIPS):
            head = 2 * lax.rem(column + slot, CHIPS) + core
            cols = pl.ds(pl.multiple_of(head * FDIM, FDIM), FDIM)
            fetch(qbuf.at[:, cols], (own, swap)[which].at[slot])
    fetch.wait()


def pack_q(queries):
    hbm = pl.BlockSpec(memory_space=pltpu.HBM)
    shape = jax.ShapeDtypeStruct((CHIPS, BLOCK, FDIM), BF16)
    return pl.pallas_call(
        pack_q_kernel,
        name="pack_q",
        out_shape=(shape, shape),
        in_specs=[hbm],
        out_specs=(hbm, hbm),
        scratch_shapes=[
            pltpu.VMEM((BLOCK, CHIPS * 2 * FDIM), BF16),
            pltpu.SemaphoreType.DMA((1,)),
            pltpu.SemaphoreType.DMA((8,)),
        ],
        compiler_params=pltpu.CompilerParams(vmem_limit_bytes=VMEM_LIMIT),
        cost_estimate=pl.CostEstimate(flops=0, bytes_accessed=8_000_000, transcendentals=0),
    )(queries)


def dot(a, b):
    return lax.dot_general(a, b, (((1,), (0,)), ((), ())), preferred_element_type=F32)


def dot_nt(a, b):
    return lax.dot_general(a, b, (((1,), (1,)), ((), ())), preferred_element_type=F32)


def update_kernel(
    bounds,
    own0,
    own1,
    own2,
    own3,
    other0,
    other1,
    other2,
    other3,
    gate_hbm,
    up_hbm,
    down_hbm,
    gate_out,
    up_out,
    down_out,
    new_gate,
    new_up,
    new_down,
    kbuf,
    vbuf,
    rbuf,
    wg,
    wu,
    wd,
    wdt,
    hid,
    dgate,
    dup,
    target,
    kt,
    tt,
    grads,
    xs,
    grams,
    sems,
    out_sems,
):
    column, parity, sequence = position()
    bound = bounds[sequence]
    fetch = Fetcher(sems)
    owns = (own0, own1, own2, own3)
    others = (other0, other1, other2, other3)
    core0, core1 = parity == 0, parity == 1

    def low_part(rows, make_dst):
        for slot in range(CHIPS):
            source = lax.rem(column + CHIPS - slot, CHIPS)
            fetch.choose(
                [(core0, owns[slot].at[rows]), (core1, others[slot].at[rows])], make_dst(source)
            )

    def top_part(rows, dst):
        options = []
        for slot in range(CHIPS):
            options.append((core0 & (column == slot), others[slot].at[rows]))
            options.append((core1 & (column == slot), owns[slot].at[rows]))
        fetch.choose(options, dst)

    def rows_at(buf):
        return lambda block: buf.at[pl.ds(pl.multiple_of(block * BLOCK, BLOCK), BLOCK)]

    fetch(gate_hbm.at[parity], wg)
    fetch(up_hbm.at[parity], wu)
    low_part(pl.ds(0, BLOCK), rows_at(kbuf))
    top_part(pl.ds(0, HALF), kbuf.at[pl.ds(CHIPS * BLOCK, HALF)])
    fetch(down_hbm.at[parity], wd)
    low_part(pl.ds(BLOCK, BLOCK), rows_at(vbuf))
    top_part(pl.ds(BLOCK, HALF), vbuf.at[pl.ds(CHIPS * BLOCK, HALF)])
    low_part(pl.ds(RATE_ROW, 16), lambda block: rbuf.at[block])
    top_part(pl.ds(RATE_ROW, 16), rbuf.at[CHIPS])
    fetch.wait()

    wdt[...] = wd[...].T
    for block in range(CHIPS + 1):
        count = min(BLOCK, HIGH - block * BLOCK)
        rows = pl.ds(block * BLOCK, count)
        rate = rbuf[block].astype(F32)[:8, :count].T[:, :1]
        place = block * BLOCK + lax.broadcasted_iota(jnp.int32, (count, 1), 0)
        weighted = rate * vbuf[rows, :].astype(F32)
        target[rows, :] = jnp.where(place < bound, weighted, 0.0).astype(BF16)
    step = 384
    for part in range(HIGH // step):
        rows = pl.ds(part * step, step)
        k_rows = kbuf[rows, :]
        t_rows = target[rows, :]
        for tile in range(HID // 256):
            cols = pl.ds(tile * 256, 256)
            pre_gate = dot(k_rows, wg[:, cols])
            pre_up = dot(k_rows, wu[:, cols])
            back = dot(t_rows, wdt[:, cols])
            logistic = 1.0 / (1.0 + jnp.exp(-pre_gate))
            act = pre_gate * logistic
            slope = logistic * (1.0 + pre_gate * (1.0 - logistic))
            hid[rows, cols] = (act * pre_up).astype(BF16)
            dgate[rows, cols] = (back * pre_up * slope).astype(BF16)
            dup[rows, cols] = (back * act).astype(BF16)
    kt[...] = kbuf[...].T
    tt[...] = target[...].T

    for which, (left, right) in enumerate(((kt, dgate), (kt, dup), (tt, hid))):
        total = jnp.zeros((1, 256), F32)
        for tile in range(HID // 256):
            cols = pl.ds(tile * 256, 256)
            grad = dot(left[...], right[:, cols])
            grads[which, :, cols] = grad
            total += jnp.sum(grad * grad, axis=0, keepdims=True)
        inv = 1.0 / jnp.sqrt(jnp.sum(total, axis=1, keepdims=True) + norm_epsilon)
        for tile in range(HID // 256):
            cols = pl.ds(tile * 256, 256)
            xs[which, :, cols] = (grads[which, :, cols] * inv).astype(BF16)

    def iteration(_, carry):
        for which in range(3):
            for tile in range(2):
                rows = pl.ds(tile * 256, 256)
                grams[which, :, rows] = dot_nt(xs[which], xs[which, rows, :]).astype(BF16)
        for which in range(3):
            gram = grams[which]
            for tile in range(2):
                cols = pl.ds(tile * 256, 256)
                mixed = cubic_coef * grams[which, :, cols].astype(F32) + quintic_coef * dot(
                    gram, grams[which, :, cols]
                )
                grams[3 + which, :, cols] = mixed.astype(BF16)
        for which in range(3):
            mix = grams[3 + which]
            for tile in range(4):
                cols = pl.ds(tile * 256, 256)
                old = xs[which, :, cols]
                xs[which, :, cols] = (linear_coef * old.astype(F32) + dot(mix, old)).astype(BF16)
        return carry

    lax.fori_loop(0, NS_ITERS, iteration, 0)

    for which, (start, out) in enumerate(((wg, new_gate), (wu, new_up))):
        for tile in range(HID // 256):
            cols = pl.ds(tile * 256, 256)
            wide = start[:, cols].astype(F32)
            moved = wide + xs[which, :, cols].astype(F32)
            aim = jnp.sqrt(jnp.sum(wide * wide, axis=0, keepdims=True) + norm_epsilon)
            actual = jnp.sqrt(jnp.sum(moved * moved, axis=0, keepdims=True) + norm_epsilon)
            out[:, cols] = (moved * (aim / actual)).astype(BF16)
    for tile in range(FDIM // 128):
        rows = pl.ds(tile * 128, 128)
        wide = wdt[rows, :].astype(F32)
        moved = wide + xs[2, rows, :].astype(F32)
        aim = jnp.sqrt(jnp.sum(wide * wide, axis=1, keepdims=True) + norm_epsilon)
        actual = jnp.sqrt(jnp.sum(moved * moved, axis=1, keepdims=True) + norm_epsilon)
        new_down[:, rows] = (moved * (aim / actual)).astype(BF16).T
    stores = Fetcher(out_sems)
    stores(new_gate, gate_out)
    stores(new_up, up_out)
    stores(new_down, down_out)
    stores.wait()


def fast_update(bounds, owns, others, starts):
    hbm = pl.BlockSpec(memory_space=pltpu.HBM)
    return pl.pallas_call(
        update_kernel,
        name="fast_update",
        out_shape=(
            jax.ShapeDtypeStruct((FDIM, HID), BF16),
            jax.ShapeDtypeStruct((FDIM, HID), BF16),
            jax.ShapeDtypeStruct((HID, FDIM), BF16),
        ),
        in_specs=[pl.BlockSpec(memory_space=pltpu.SMEM)] + [hbm] * 11,
        out_specs=(hbm, hbm, hbm),
        scratch_shapes=[
            pltpu.VMEM((FDIM, HID), BF16),
            pltpu.VMEM((FDIM, HID), BF16),
            pltpu.VMEM((HID, FDIM), BF16),
            pltpu.VMEM((HIGH, FDIM), BF16),
            pltpu.VMEM((HIGH, FDIM), BF16),
            pltpu.VMEM((CHIPS + 1, 16, FDIM), BF16),
            pltpu.VMEM((FDIM, HID), BF16),
            pltpu.VMEM((FDIM, HID), BF16),
            pltpu.VMEM((HID, FDIM), BF16),
            pltpu.VMEM((FDIM, HID), BF16),
            pltpu.VMEM((HIGH, HID), BF16),
            pltpu.VMEM((HIGH, HID), BF16),
            pltpu.VMEM((HIGH, HID), BF16),
            pltpu.VMEM((HIGH, FDIM), BF16),
            pltpu.VMEM((FDIM, HIGH), BF16),
            pltpu.VMEM((FDIM, HIGH), BF16),
            pltpu.VMEM((3, FDIM, HID), F32),
            pltpu.VMEM((3, FDIM, HID), BF16),
            pltpu.VMEM((6, FDIM, FDIM), BF16),
            pltpu.SemaphoreType.DMA((18,)),
            pltpu.SemaphoreType.DMA((3,)),
        ],
        compiler_params=pltpu.CompilerParams(vmem_limit_bytes=VMEM_LIMIT),
        cost_estimate=pl.CostEstimate(
            flops=20_000_000_000, bytes_accessed=12_000_000, transcendentals=1_200_000
        ),
    )(bounds, *owns, *others, *starts)


def apply_kernel(
    chunk,
    bounds,
    own_q,
    other_q,
    q1,
    q2,
    q3,
    own0,
    own1,
    own2,
    own3,
    other0,
    other1,
    other2,
    other3,
    halo,
    gate_hbm,
    up_hbm,
    down_hbm,
    gate_new,
    up_new,
    down_new,
    gain_hbm,
    out_hbm,
    out,
    qc,
    kbuf,
    vbuf,
    wg,
    wu,
    wd,
    new_gate,
    new_up,
    new_down,
    gain,
    hid,
    raw,
    before,
    fast,
    sems,
    out_sem,
):
    column, parity, sequence = position()
    bound = bounds[sequence]
    owned = 2 * column + parity
    fetch = Fetcher(sems)

    def q_rows_of(core, source):
        return qc.at[pl.ds(pl.multiple_of((core * CHIPS + source) * HALF, HALF), HALF)]

    def sender(slot):
        return lax.rem(column + CHIPS - slot, CHIPS)

    fetch(gate_hbm.at[parity], wg)
    fetch(up_hbm.at[parity], wu)
    q_src = pl.ds(chunk * HALF, HALF)
    fetch(own_q.at[0, q_src], q_rows_of(parity, column))
    fetch(other_q.at[0, q_src], q_rows_of(1 - parity, column))
    for slot, array in ((1, q1), (2, q2), (3, q3)):
        fetch(array.at[q_src], q_rows_of(parity, sender(slot)))
        fetch(array.at[pl.ds(BLOCK + chunk * HALF, HALF)], q_rows_of(1 - parity, sender(slot)))
    early = len(fetch.copies)
    fetch(down_hbm.at[parity], wd)
    downs = len(fetch.copies)
    fetch(gate_new, new_gate)
    fetch(up_new, new_up)
    fetch(down_new, new_down)
    fetch(gain_hbm, gain)
    first = len(fetch.copies)
    fetch.wait(0, early)
    for which, buf in ((0, kbuf), (1, vbuf)):
        rows = pl.ds(which * BLOCK, BLOCK)

        def rows_at(core, source, buf=buf):
            start = WINDOW + (core * CHIPS + source) * BLOCK
            return buf.at[pl.ds(pl.multiple_of(start, BLOCK), BLOCK)]

        fetch(halo.at[pl.ds(which * WINDOW, WINDOW)], buf.at[pl.ds(0, WINDOW)])
        for slot, own, other in (
            (0, own0, other0),
            (1, own1, other1),
            (2, own2, other2),
            (3, own3, other3),
        ):
            fetch(own.at[rows], rows_at(parity, sender(slot)))
            fetch(other.at[rows], rows_at(1 - parity, sender(slot)))

    def swiglu(rows, gate, up, down, store, ready):
        in_rows = qc[rows, :]
        for tile in range(HID // 256):
            cols = pl.ds(tile * 256, 256)
            pre_gate = dot(in_rows, gate[:, cols])
            pre_up = dot(in_rows, up[:, cols])
            hid[pl.ds(0, rows.size), cols] = (
                pre_gate / (1.0 + jnp.exp(-pre_gate)) * pre_up
            ).astype(BF16)
        ready()
        store(dot(hid[pl.ds(0, rows.size), :], down[...]))

    edge = 4 if chunk == 0 else 3
    old_rows = pl.ds(0, (edge + 1) * HALF)
    new_rows = pl.ds(edge * HALF, (SPLIT - edge) * HALF)

    def store_old(value):
        raw[pl.ds(0, edge * HALF), :] = value[: edge * HALF]
        before[...] = value[edge * HALF :]

    def store_new(value):
        raw[new_rows, :] = value

    swiglu(old_rows, wg, wu, wd, store_old, lambda: fetch.wait(early, downs))
    fetch.wait(downs, first)
    swiglu(new_rows, new_gate, new_up, new_down, store_new, lambda: None)
    mid = pl.ds(edge * HALF, HALF)
    place = edge * BLOCK + chunk * HALF + lax.broadcasted_iota(jnp.int32, (HALF, 1), 0)
    raw[mid, :] = jnp.where(place < bound, before[...], raw[mid, :])
    gain_row = gain[pl.ds(owned, 1), :]
    for block in range(SPLIT):
        rows = pl.ds(block * HALF, HALF)
        value = raw[rows, :]
        root = jnp.sqrt(jnp.mean(value * value, axis=1, keepdims=True) + rms_epsilon)
        fast[rows, :] = (value / root * gain_row).astype(BF16)
    fetch.wait(first)

    row_iota = lax.broadcasted_iota(jnp.int32, (HALF, HALF), 0)
    col_iota = lax.broadcasted_iota(jnp.int32, (HALF, HALF), 1)
    keep_old = col_iota > row_iota
    keep_own = col_iota <= row_iota

    def attend(block, edge_block):
        base = pl.multiple_of(block * BLOCK + chunk * HALF, HALF)
        q_rows = pl.ds(pl.multiple_of(block * HALF, HALF), HALF)
        o_rows = pl.ds(pl.multiple_of(place_of(block) * HALF, HALF), HALF)
        keys = pl.ds(base, WINDOW + HALF)
        for head in range(FDIM // AHD):
            cols = pl.ds(head * AHD, AHD)
            scores = dot_nt(qc[q_rows, cols], kbuf[keys, cols])
            parts = [scores[:, i * HALF : (i + 1) * HALF] for i in range(5)]
            parts[0] = jnp.where(keep_old, parts[0], MASKED)
            parts[4] = jnp.where(keep_own, parts[4], MASKED)
            if edge_block:
                for i in range(4):
                    absent = (sequence == 0) & (base + i * HALF < WINDOW)
                    parts[i] = jnp.where(absent, MASKED, parts[i])
            masked = jnp.concatenate(parts, axis=1)
            top = jnp.max(masked, axis=1, keepdims=True)
            weights = jnp.exp2((masked - top) * EXP2_SCALE)
            total = jnp.sum(weights, axis=1, keepdims=True)
            mixed = dot(weights.astype(BF16), vbuf[keys, cols])
            attn = (mixed / total).astype(BF16)
            out[o_rows, cols] = (attn.astype(F32) + fast[q_rows, cols].astype(F32)).astype(BF16)

    def edge_body(block, carry):
        attend(block, True)
        return carry

    def main_body(block, carry):
        attend(block, False)
        return carry

    lax.fori_loop(0, 2, edge_body, 0)
    lax.fori_loop(2, SPLIT, main_body, 0)
    copy = pltpu.make_async_copy(out, out_hbm, out_sem)
    copy.start()
    copy.wait()


def apply_chunk(chunk, bounds, local_q, q_parts, owns, others, halo, starts, news, gain):
    hbm = pl.BlockSpec(memory_space=pltpu.HBM)
    rows = SPLIT * HALF
    return pl.pallas_call(
        functools.partial(apply_kernel, chunk),
        name="apply_attend",
        out_shape=jax.ShapeDtypeStruct((rows, FDIM), BF16),
        in_specs=[pl.BlockSpec(memory_space=pltpu.SMEM)] + [hbm] * 21,
        out_specs=hbm,
        scratch_shapes=[
            pltpu.VMEM((rows, FDIM), BF16),
            pltpu.VMEM((rows, FDIM), BF16),
            pltpu.VMEM((WINDOW + LEN, FDIM), BF16),
            pltpu.VMEM((WINDOW + LEN, FDIM), BF16),
            pltpu.VMEM((FDIM, HID), BF16),
            pltpu.VMEM((FDIM, HID), BF16),
            pltpu.VMEM((HID, FDIM), BF16),
            pltpu.VMEM((FDIM, HID), BF16),
            pltpu.VMEM((FDIM, HID), BF16),
            pltpu.VMEM((HID, FDIM), BF16),
            pltpu.VMEM((SPLIT, FDIM), F32),
            pltpu.VMEM((5 * HALF, HID), BF16),
            pltpu.VMEM((rows, FDIM), F32),
            pltpu.VMEM((HALF, FDIM), F32),
            pltpu.VMEM((rows, FDIM), BF16),
            pltpu.SemaphoreType.DMA((33,)),
            pltpu.SemaphoreType.DMA,
        ],
        compiler_params=pltpu.CompilerParams(vmem_limit_bytes=VMEM_LIMIT),
        cost_estimate=pl.CostEstimate(
            flops=8_000_000_000, bytes_accessed=14_000_000, transcendentals=4_000_000
        ),
    )(bounds, *local_q, *q_parts, *owns, *others, halo, *starts, *news, gain)


def body(queries, keys, values, token_rates, gate_start, up_start, down_start, norm_gain, bounds):
    shards = lax.axis_size("tok") * lax.axis_size("head")
    column = lax.axis_index("head")
    parity = lax.axis_index("tok") % 2
    groups = [
        [s * SPLIT + place for place in sorted(range(SPLIT), key=lambda b: (b % CHIPS, b // CHIPS))]
        for s in range(shards // SPLIT)
    ]
    tok_count = lax.axis_size("tok")

    def across_core(array):
        return lax.ppermute(array, "tok", [(i, i ^ 1) for i in range(tok_count)])

    def along(array, slot):
        return lax.ppermute(array, "head", [(i, (i + slot) % CHIPS) for i in range(CHIPS)])

    def next_segment(array):
        return lax.ppermute(array, "tok", [(i, i + 2) for i in range(tok_count - 2)])

    order = (1, 3, 2)
    own_kv, swap_kv = pack_kv(keys, values, token_rates.T)
    other_kv = across_core(swap_kv)
    owns, others = [own_kv[0]] * CHIPS, [other_kv[0]] * CHIPS
    for slot in order:
        owns[slot] = along(own_kv[slot], slot)
    queries, owns[0] = lax.optimization_barrier((queries, owns[0]))
    own_q, swap_q = pack_q(queries)
    other_q = across_core(swap_q)
    for slot in order:
        others[slot] = along(other_kv[slot], slot)
    q_parts = [None] * CHIPS
    for slot in order:
        part = jnp.concatenate([own_q[slot], other_q[slot]], axis=0)
        others[slot], part = lax.optimization_barrier((others[slot], part))
        q_parts[slot] = along(part, slot)

    first_core = parity == 0

    def tail(source):
        value = jnp.where(first_core, others[0], owns[0])
        for slot in order:
            here = jnp.where(first_core, others[slot], owns[slot])
            value = jnp.where(column == (source + slot) % CHIPS, here, value)
        return value

    tails = [tail(source) for source in (2, 3)]
    halo = next_segment(
        jnp.concatenate(
            [t[part * BLOCK : (part + 1) * BLOCK] for part in range(2) for t in tails], axis=0
        )
    )

    starts = (gate_start, up_start, down_start)
    news = fast_update(bounds, owns, others, starts)
    gain = norm_gain.reshape(-1, FDIM)
    returned = []
    for chunk in range(2):
        out = apply_chunk(
            chunk,
            bounds,
            (own_q, other_q),
            q_parts[1:],
            owns,
            others,
            halo,
            starts,
            news,
            gain,
        )
        returned.append(
            lax.all_to_all(
                out, AXES, split_axis=0, concat_axis=1, tiled=True, axis_index_groups=groups
            )
        )
    return jnp.concatenate(returned, axis=0)


def solution(mesh):
    tokens = P(AXES, None)
    return jax.shard_map(
        body,
        mesh=mesh,
        in_specs=(
            tokens,
            tokens,
            tokens,
            tokens,
            P("head", None, None),
            P("head", None, None),
            P("head", None, None),
            P(),
            P(),
        ),
        out_specs=tokens,
        check_vma=False,
    )
```

```python
import functools
import math

import jax
import jax.numpy as jnp
from jax import lax
from jax.experimental import pallas as pl
from jax.experimental.pallas import tpu as pltpu
from jax.sharding import PartitionSpec as P

FDIM = 512
HID = 1024
AHD = 128
WINDOW = 512
NS_ITERS = 3
LEN = 2048
HALF = 128
LOW = 896
HIGH = 1152
SPLIT = 8
BLOCK = LEN // SPLIT

linear_coef = 3.4445
cubic_coef = -4.775
quintic_coef = 2.0315
rms_epsilon = 1e-05
norm_epsilon = 1e-06
MASKED = -1e30
EXP2_SCALE = math.log2(math.e) / math.sqrt(AHD)

AXES = ("tok", "head")
F32 = jnp.float32
BF16 = jnp.bfloat16


CHIPS = 4
KV_ROWS = 528
RATE_ROW = 512
VMEM_LIMIT = 60 * 1024 * 1024


def place_of(block):
    return (block % CHIPS) * 2 + block // CHIPS


class Fetcher:
    def __init__(self, sems):
        self.sems = sems
        self.copies = []

    def __call__(self, src, dst):
        copy = pltpu.make_async_copy(src, dst, self.sems.at[len(self.copies)])
        copy.start()
        self.copies.append(copy)

    def choose(self, options, dst):
        sem = self.sems.at[len(self.copies)]
        for cond, src in options:

            @pl.when(cond)
            def _(src=src):
                pltpu.make_async_copy(src, dst, sem).start()

        self.copies.append(pltpu.make_async_copy(options[0][1], dst, sem))

    def wait(self, first=0, last=None):
        for copy in self.copies[first:last]:
            copy.wait()


def position():
    column = lax.axis_index("head")
    tok = lax.axis_index("tok")
    return column, lax.rem(tok, 2), lax.div(tok, 2)


def pack_kernel(keys, values, queries, rates, *rest):
    kv_outs = rest[: 2 * CHIPS]
    q_out, q_swap = rest[2 * CHIPS : 2 * CHIPS + 2]
    kbuf, vbuf, qbuf, lines, in_sems, sems = rest[2 * CHIPS + 2 :]
    column, parity, _ = position()
    load = Fetcher(in_sems)
    fetch = Fetcher(sems)
    load(keys, kbuf)
    load(values, vbuf)
    load(queries, qbuf)
    turned = rates[...].astype(F32)
    place = lax.broadcasted_iota(jnp.int32, turned.shape, 0)
    targets = []
    for which in range(2):
        core = parity if which == 0 else 1 - parity
        for slot in range(CHIPS):
            head = 2 * lax.rem(column + slot, CHIPS) + core
            targets.append((which * CHIPS + slot, head))
    for index, head in targets:
        line = jnp.sum(jnp.where(place == head, turned, 0.0), axis=0, keepdims=True)
        lines[index, :, pl.ds(0, BLOCK)] = jnp.broadcast_to(line, (16, BLOCK)).astype(BF16)
        lines[index, :, pl.ds(BLOCK, FDIM - BLOCK)] = jnp.zeros((16, FDIM - BLOCK), BF16)
    for index, head in targets:
        fetch(lines.at[index], kv_outs[index].at[pl.ds(RATE_ROW, 16)])
    for part, buf in ((0, kbuf), (1, vbuf), (2, qbuf)):
        load.wait(part, part + 1)
        for index, head in targets:
            cols = pl.ds(pl.multiple_of(head * FDIM, FDIM), FDIM)
            if part < 2:
                dst = kv_outs[index].at[pl.ds(part * BLOCK, BLOCK)]
            else:
                dst = (q_out, q_swap)[index // CHIPS].at[index % CHIPS]
            fetch(buf.at[:, cols], dst)
    fetch.wait()


def pack(keys, values, queries, rates):
    hbm = pl.BlockSpec(memory_space=pltpu.HBM)
    kv_shape = jax.ShapeDtypeStruct((KV_ROWS, FDIM), BF16)
    q_shape = jax.ShapeDtypeStruct((CHIPS, BLOCK, FDIM), BF16)
    width = CHIPS * 2 * FDIM
    outs = pl.pallas_call(
        pack_kernel,
        name="pack",
        out_shape=(kv_shape,) * (2 * CHIPS) + (q_shape, q_shape),
        in_specs=[hbm, hbm, hbm, pl.BlockSpec(memory_space=pltpu.VMEM)],
        out_specs=(hbm,) * (2 * CHIPS + 2),
        scratch_shapes=[
            pltpu.VMEM((BLOCK, width), BF16),
            pltpu.VMEM((BLOCK, width), BF16),
            pltpu.VMEM((BLOCK, width), BF16),
            pltpu.VMEM((2 * CHIPS, 16, FDIM), BF16),
            pltpu.SemaphoreType.DMA((3,)),
            pltpu.SemaphoreType.DMA((32,)),
        ],
        compiler_params=pltpu.CompilerParams(vmem_limit_bytes=VMEM_LIMIT),
        cost_estimate=pl.CostEstimate(flops=0, bytes_accessed=24_000_000, transcendentals=0),
    )(keys, values, queries, rates)
    return outs[:CHIPS], outs[CHIPS : 2 * CHIPS], *outs[2 * CHIPS :]


def dot(a, b):
    return lax.dot_general(a, b, (((1,), (0,)), ((), ())), preferred_element_type=F32)


def dot_nt(a, b):
    return lax.dot_general(a, b, (((1,), (1,)), ((), ())), preferred_element_type=F32)


def update_kernel(
    bounds,
    own0,
    own1,
    own2,
    own3,
    other0,
    other1,
    other2,
    other3,
    gate_hbm,
    up_hbm,
    down_hbm,
    gate_out,
    up_out,
    down_out,
    new_gate,
    new_up,
    new_down,
    kbuf,
    vbuf,
    rbuf,
    wg,
    wu,
    wd,
    wdt,
    hid,
    dgate,
    dup,
    target,
    kt,
    tt,
    grads,
    xs,
    grams,
    sems,
    out_sems,
):
    column, parity, sequence = position()
    bound = bounds[sequence]
    fetch = Fetcher(sems)
    owns = (own0, own1, own2, own3)
    others = (other0, other1, other2, other3)
    core0, core1 = parity == 0, parity == 1

    def low_part(rows, make_dst):
        for slot in range(CHIPS):
            source = lax.rem(column + CHIPS - slot, CHIPS)
            fetch.choose(
                [(core0, owns[slot].at[rows]), (core1, others[slot].at[rows])], make_dst(source)
            )

    def top_part(rows, dst):
        options = []
        for slot in range(CHIPS):
            options.append((core0 & (column == slot), others[slot].at[rows]))
            options.append((core1 & (column == slot), owns[slot].at[rows]))
        fetch.choose(options, dst)

    def rows_at(buf):
        return lambda block: buf.at[pl.ds(pl.multiple_of(block * BLOCK, BLOCK), BLOCK)]

    fetch(down_hbm.at[parity], wd)
    low_part(pl.ds(0, BLOCK), rows_at(kbuf))
    top_part(pl.ds(0, HALF), kbuf.at[pl.ds(CHIPS * BLOCK, HALF)])
    low_part(pl.ds(BLOCK, BLOCK), rows_at(vbuf))
    top_part(pl.ds(BLOCK, HALF), vbuf.at[pl.ds(CHIPS * BLOCK, HALF)])
    low_part(pl.ds(RATE_ROW, 16), lambda block: rbuf.at[block])
    top_part(pl.ds(RATE_ROW, 16), rbuf.at[CHIPS])
    fetch(gate_hbm.at[parity], wg)
    fetch(up_hbm.at[parity], wu)
    fetch.wait(0, 1)
    wdt[...] = wd[...].T
    fetch.wait(1, 6)
    kt[...] = kbuf[...].T
    fetch.wait(6, 16)
    for block in range(CHIPS + 1):
        count = min(BLOCK, HIGH - block * BLOCK)
        rows = pl.ds(block * BLOCK, count)
        rate = rbuf[block].astype(F32)[:8, :count].T[:, :1]
        place = block * BLOCK + lax.broadcasted_iota(jnp.int32, (count, 1), 0)
        weighted = rate * vbuf[rows, :].astype(F32)
        target[rows, :] = jnp.where(place < bound, weighted, 0.0).astype(BF16)
    tt[...] = target[...].T
    fetch.wait(16)
    step = 384
    for part in range(HIGH // step):
        rows = pl.ds(part * step, step)
        k_rows = kbuf[rows, :]
        t_rows = target[rows, :]
        for tile in range(HID // 256):
            cols = pl.ds(tile * 256, 256)
            pre_gate = dot(k_rows, wg[:, cols])
            pre_up = dot(k_rows, wu[:, cols])
            back = dot(t_rows, wdt[:, cols])
            logistic = 1.0 / (1.0 + jnp.exp(-pre_gate))
            act = pre_gate * logistic
            slope = logistic * (1.0 + pre_gate * (1.0 - logistic))
            hid[rows, cols] = (act * pre_up).astype(BF16)
            dgate[rows, cols] = (back * pre_up * slope).astype(BF16)
            dup[rows, cols] = (back * act).astype(BF16)

    for which, (left, right) in enumerate(((kt, dgate), (kt, dup), (tt, hid))):
        total = jnp.zeros((1, 256), F32)
        for tile in range(HID // 256):
            cols = pl.ds(tile * 256, 256)
            grad = dot(left[...], right[:, cols])
            grads[which, :, cols] = grad
            total += jnp.sum(grad * grad, axis=0, keepdims=True)
        inv = 1.0 / jnp.sqrt(jnp.sum(total, axis=1, keepdims=True) + norm_epsilon)
        for tile in range(HID // 256):
            cols = pl.ds(tile * 256, 256)
            xs[which, :, cols] = (grads[which, :, cols] * inv).astype(BF16)

    def iteration(_, carry):
        for which in range(3):
            for tile in range(2):
                rows = pl.ds(tile * 256, 256)
                grams[which, :, rows] = dot_nt(xs[which], xs[which, rows, :]).astype(BF16)
        for which in range(3):
            gram = grams[which]
            for tile in range(2):
                cols = pl.ds(tile * 256, 256)
                mixed = cubic_coef * grams[which, :, cols].astype(F32) + quintic_coef * dot(
                    gram, grams[which, :, cols]
                )
                grams[3 + which, :, cols] = mixed.astype(BF16)
        for which in range(3):
            mix = grams[3 + which]
            for tile in range(4):
                cols = pl.ds(tile * 256, 256)
                old = xs[which, :, cols]
                xs[which, :, cols] = (linear_coef * old.astype(F32) + dot(mix, old)).astype(BF16)
        return carry

    lax.fori_loop(0, NS_ITERS, iteration, 0)

    stores = Fetcher(out_sems)
    for which, (start, out, target_hbm) in enumerate(
        ((wg, new_gate, gate_out), (wu, new_up, up_out))
    ):
        for tile in range(HID // 256):
            cols = pl.ds(tile * 256, 256)
            wide = start[:, cols].astype(F32)
            moved = wide + xs[which, :, cols].astype(F32)
            aim = jnp.sqrt(jnp.sum(wide * wide, axis=0, keepdims=True) + norm_epsilon)
            actual = jnp.sqrt(jnp.sum(moved * moved, axis=0, keepdims=True) + norm_epsilon)
            out[:, cols] = (moved * (aim / actual)).astype(BF16)
        stores(out, target_hbm)
    for tile in range(FDIM // 128):
        rows = pl.ds(tile * 128, 128)
        wide = wdt[rows, :].astype(F32)
        moved = wide + xs[2, rows, :].astype(F32)
        aim = jnp.sqrt(jnp.sum(wide * wide, axis=1, keepdims=True) + norm_epsilon)
        actual = jnp.sqrt(jnp.sum(moved * moved, axis=1, keepdims=True) + norm_epsilon)
        new_down[rows, :] = (moved * (aim / actual)).astype(BF16)
    stores(new_down, down_out)
    stores.wait()


def fast_update(bounds, owns, others, starts):
    hbm = pl.BlockSpec(memory_space=pltpu.HBM)
    return pl.pallas_call(
        update_kernel,
        name="fast_update",
        out_shape=(
            jax.ShapeDtypeStruct((FDIM, HID), BF16),
            jax.ShapeDtypeStruct((FDIM, HID), BF16),
            jax.ShapeDtypeStruct((FDIM, HID), BF16),
        ),
        in_specs=[pl.BlockSpec(memory_space=pltpu.SMEM)] + [hbm] * 11,
        out_specs=(hbm, hbm, hbm),
        scratch_shapes=[
            pltpu.VMEM((FDIM, HID), BF16),
            pltpu.VMEM((FDIM, HID), BF16),
            pltpu.VMEM((FDIM, HID), BF16),
            pltpu.VMEM((HIGH, FDIM), BF16),
            pltpu.VMEM((HIGH, FDIM), BF16),
            pltpu.VMEM((CHIPS + 1, 16, FDIM), BF16),
            pltpu.VMEM((FDIM, HID), BF16),
            pltpu.VMEM((FDIM, HID), BF16),
            pltpu.VMEM((HID, FDIM), BF16),
            pltpu.VMEM((FDIM, HID), BF16),
            pltpu.VMEM((HIGH, HID), BF16),
            pltpu.VMEM((HIGH, HID), BF16),
            pltpu.VMEM((HIGH, HID), BF16),
            pltpu.VMEM((HIGH, FDIM), BF16),
            pltpu.VMEM((FDIM, HIGH), BF16),
            pltpu.VMEM((FDIM, HIGH), BF16),
            pltpu.VMEM((3, FDIM, HID), F32),
            pltpu.VMEM((3, FDIM, HID), BF16),
            pltpu.VMEM((6, FDIM, FDIM), BF16),
            pltpu.SemaphoreType.DMA((18,)),
            pltpu.SemaphoreType.DMA((3,)),
        ],
        compiler_params=pltpu.CompilerParams(vmem_limit_bytes=VMEM_LIMIT),
        cost_estimate=pl.CostEstimate(
            flops=20_000_000_000, bytes_accessed=12_000_000, transcendentals=1_200_000
        ),
    )(bounds, *owns, *others, *starts)


def apply_kernel(
    chunk,
    bounds,
    own_q,
    other_q,
    q1,
    q2,
    q3,
    own0,
    own1,
    own2,
    own3,
    other0,
    other1,
    other2,
    other3,
    halo,
    gate_hbm,
    up_hbm,
    down_hbm,
    gate_new,
    up_new,
    down_new,
    gain_hbm,
    out_hbm,
    out,
    qc,
    kbuf,
    vbuf,
    wg,
    wu,
    wd,
    new_gate,
    new_up,
    new_down,
    gain,
    hid,
    raw,
    before,
    fast,
    sems,
    out_sem,
    scores,
    rounded,
):
    column, parity, sequence = position()
    bound = bounds[sequence]
    owned = 2 * column + parity
    fetch = Fetcher(sems)

    def q_rows_of(core, source):
        return qc.at[pl.ds(pl.multiple_of((core * CHIPS + source) * HALF, HALF), HALF)]

    def sender(slot):
        return lax.rem(column + CHIPS - slot, CHIPS)

    fetch(gate_hbm.at[parity], wg)
    fetch(up_hbm.at[parity], wu)
    q_src = pl.ds(chunk * HALF, HALF)
    fetch(own_q.at[0, q_src], q_rows_of(parity, column))
    fetch(other_q.at[0, q_src], q_rows_of(1 - parity, column))
    for slot, array in ((1, q1), (2, q2), (3, q3)):
        fetch(array.at[q_src], q_rows_of(parity, sender(slot)))
        fetch(array.at[pl.ds(BLOCK + chunk * HALF, HALF)], q_rows_of(1 - parity, sender(slot)))
    early = len(fetch.copies)
    fetch(down_hbm.at[parity], wd)
    downs = len(fetch.copies)
    fetch(gate_new, new_gate)
    fetch(up_new, new_up)
    fetch(down_new, new_down)
    fetch(gain_hbm, gain)
    first = len(fetch.copies)
    fetch.wait(0, early)
    for which, buf in ((0, kbuf), (1, vbuf)):
        rows = pl.ds(which * BLOCK, BLOCK)

        def rows_at(core, source, buf=buf):
            start = WINDOW + (core * CHIPS + source) * BLOCK
            return buf.at[pl.ds(pl.multiple_of(start, BLOCK), BLOCK)]

        fetch(halo.at[pl.ds(which * WINDOW, WINDOW)], buf.at[pl.ds(0, WINDOW)])
        for slot, own, other in (
            (0, own0, other0),
            (1, own1, other1),
            (2, own2, other2),
            (3, own3, other3),
        ):
            fetch(own.at[rows], rows_at(parity, sender(slot)))
            fetch(other.at[rows], rows_at(1 - parity, sender(slot)))

    def swiglu(rows, gate, up, down, product, store, ready):
        in_rows = qc[rows, :]
        for tile in range(HID // 256):
            cols = pl.ds(tile * 256, 256)
            pre_gate = dot(in_rows, gate[:, cols])
            pre_up = dot(in_rows, up[:, cols])
            hid[pl.ds(0, rows.size), cols] = (
                pre_gate / (1.0 + jnp.exp(-pre_gate)) * pre_up
            ).astype(BF16)
        ready()
        store(product(hid[pl.ds(0, rows.size), :], down[...]))

    edge = 4 if chunk == 0 else 3
    old_rows = pl.ds(0, (edge + 1) * HALF)
    new_rows = pl.ds(edge * HALF, (SPLIT - edge) * HALF)

    def store_old(value):
        raw[pl.ds(0, edge * HALF), :] = value[: edge * HALF]
        before[...] = value[edge * HALF :]

    def store_new(value):
        raw[new_rows, :] = value

    swiglu(old_rows, wg, wu, wd, dot, store_old, lambda: fetch.wait(early, downs))
    fetch.wait(downs, first)
    swiglu(new_rows, new_gate, new_up, new_down, dot_nt, store_new, lambda: None)
    mid = pl.ds(edge * HALF, HALF)
    place = edge * BLOCK + chunk * HALF + lax.broadcasted_iota(jnp.int32, (HALF, 1), 0)
    raw[mid, :] = jnp.where(place < bound, before[...], raw[mid, :])
    gain_row = gain[pl.ds(owned, 1), :]
    for block in range(SPLIT):
        rows = pl.ds(block * HALF, HALF)
        value = raw[rows, :]
        root = jnp.sqrt(jnp.mean(value * value, axis=1, keepdims=True) + rms_epsilon)
        fast[rows, :] = (value / root * gain_row).astype(BF16)
    fetch.wait(first)

    row_iota = lax.broadcasted_iota(jnp.int32, (HALF, HALF), 0)
    col_iota = lax.broadcasted_iota(jnp.int32, (HALF, HALF), 1)
    keep_old = col_iota > row_iota
    keep_own = col_iota <= row_iota

    def attend(block, edge_block):
        base = pl.multiple_of(block * BLOCK + chunk * HALF, HALF)
        q_rows = pl.ds(pl.multiple_of(block * HALF, HALF), HALF)
        o_rows = pl.ds(pl.multiple_of(place_of(block) * HALF, HALF), HALF)
        keys = pl.ds(base, WINDOW + HALF)
        heads = range(FDIM // AHD)
        for head in heads:
            cols = pl.ds(head * AHD, AHD)
            scores[head] = dot_nt(qc[q_rows, cols], kbuf[keys, cols])
        totals = []
        for head in heads:
            parts = [scores[head, :, i * HALF : (i + 1) * HALF] for i in range(5)]
            parts[0] = jnp.where(keep_old, parts[0], MASKED)
            parts[4] = jnp.where(keep_own, parts[4], MASKED)
            if edge_block:
                for i in range(4):
                    absent = (sequence == 0) & (base + i * HALF < WINDOW)
                    parts[i] = jnp.where(absent, MASKED, parts[i])
            top = jnp.max(functools.reduce(jnp.maximum, parts), axis=1, keepdims=True)
            total = None
            for i in range(5):
                weight = jnp.exp2((parts[i] - top) * EXP2_SCALE)
                rounded[head, :, i * HALF : (i + 1) * HALF] = weight.astype(BF16)
                total = weight if total is None else total + weight
            totals.append(jnp.sum(total, axis=1, keepdims=True))
        for head in heads:
            cols = pl.ds(head * AHD, AHD)
            mixed = dot(rounded[head], vbuf[keys, cols])
            attn = (mixed / totals[head]).astype(BF16)
            out[o_rows, cols] = (attn.astype(F32) + fast[q_rows, cols].astype(F32)).astype(BF16)

    def edge_body(block, carry):
        attend(block, True)
        return carry

    def main_body(block, carry):
        attend(block, False)
        return carry

    lax.fori_loop(0, 2, edge_body, 0, unroll=2)
    lax.fori_loop(2, SPLIT, main_body, 0, unroll=2)
    copy = pltpu.make_async_copy(out, out_hbm, out_sem)
    copy.start()
    copy.wait()


def apply_chunk(chunk, bounds, local_q, q_parts, owns, others, halo, starts, news, gain):
    hbm = pl.BlockSpec(memory_space=pltpu.HBM)
    rows = SPLIT * HALF
    return pl.pallas_call(
        functools.partial(apply_kernel, chunk),
        name="apply_attend",
        out_shape=jax.ShapeDtypeStruct((rows, FDIM), BF16),
        in_specs=[pl.BlockSpec(memory_space=pltpu.SMEM)] + [hbm] * 21,
        out_specs=hbm,
        scratch_shapes=[
            pltpu.VMEM((rows, FDIM), BF16),
            pltpu.VMEM((rows, FDIM), BF16),
            pltpu.VMEM((WINDOW + LEN, FDIM), BF16),
            pltpu.VMEM((WINDOW + LEN, FDIM), BF16),
            pltpu.VMEM((FDIM, HID), BF16),
            pltpu.VMEM((FDIM, HID), BF16),
            pltpu.VMEM((HID, FDIM), BF16),
            pltpu.VMEM((FDIM, HID), BF16),
            pltpu.VMEM((FDIM, HID), BF16),
            pltpu.VMEM((FDIM, HID), BF16),
            pltpu.VMEM((SPLIT, FDIM), F32),
            pltpu.VMEM((5 * HALF, HID), BF16),
            pltpu.VMEM((rows, FDIM), F32),
            pltpu.VMEM((HALF, FDIM), F32),
            pltpu.VMEM((rows, FDIM), BF16),
            pltpu.SemaphoreType.DMA((33,)),
            pltpu.SemaphoreType.DMA,
            pltpu.VMEM((FDIM // AHD, HALF, WINDOW + HALF), F32),
            pltpu.VMEM((FDIM // AHD, HALF, WINDOW + HALF), BF16),
        ],
        compiler_params=pltpu.CompilerParams(vmem_limit_bytes=VMEM_LIMIT),
        cost_estimate=pl.CostEstimate(
            flops=8_000_000_000, bytes_accessed=14_000_000, transcendentals=4_000_000
        ),
    )(bounds, *local_q, *q_parts, *owns, *others, halo, *starts, *news, gain)


def body(queries, keys, values, token_rates, gate_start, up_start, down_start, norm_gain, bounds):
    shards = lax.axis_size("tok") * lax.axis_size("head")
    column = lax.axis_index("head")
    parity = lax.axis_index("tok") % 2
    groups = [
        [s * SPLIT + place for place in sorted(range(SPLIT), key=lambda b: (b % CHIPS, b // CHIPS))]
        for s in range(shards // SPLIT)
    ]
    tok_count = lax.axis_size("tok")

    def along(array, slot):
        return lax.ppermute(array, "head", [(i, (i + slot) % CHIPS) for i in range(CHIPS)])

    def across(array, slot):
        pairs = [
            (t * CHIPS + i, (t ^ 1) * CHIPS + (i + slot) % CHIPS)
            for t in range(tok_count)
            for i in range(CHIPS)
        ]
        return lax.ppermute(array, AXES, pairs)

    def next_segment(array):
        return lax.ppermute(array, "tok", [(i, i + 2) for i in range(tok_count - 2)])

    order = (1, 3, 2)
    own_kv, swap_kv, own_q, swap_q = pack(keys, values, queries, token_rates.T)
    owns, others = [own_kv[0]] * CHIPS, [None] * CHIPS
    for slot in order:
        owns[slot] = along(own_kv[slot], slot)
    for slot in order + (0,):
        others[slot] = across(swap_kv[slot], slot)
    other_q = across(swap_q, 0)
    q_parts = [None] * CHIPS
    for slot in order:
        part = jnp.concatenate([own_q[slot], other_q[slot]], axis=0)
        others[slot], part = lax.optimization_barrier((others[slot], part))
        q_parts[slot] = along(part, slot)

    first_core = parity == 0

    def tail(source):
        value = jnp.where(first_core, others[0], owns[0])
        for slot in order:
            here = jnp.where(first_core, others[slot], owns[slot])
            value = jnp.where(column == (source + slot) % CHIPS, here, value)
        return value

    tails = [tail(source) for source in (2, 3)]
    halo = next_segment(
        jnp.concatenate(
            [t[part * BLOCK : (part + 1) * BLOCK] for part in range(2) for t in tails], axis=0
        )
    )

    starts = (gate_start, up_start, down_start)
    news = fast_update(bounds, owns, others, starts)
    gain = norm_gain.reshape(-1, FDIM)
    returned = []
    for chunk in range(2):
        out = apply_chunk(
            chunk,
            bounds,
            (own_q, other_q),
            q_parts[1:],
            owns,
            others,
            halo,
            starts,
            news,
            gain,
        )
        returned.append(
            lax.all_to_all(
                out, AXES, split_axis=0, concat_axis=1, tiled=True, axis_index_groups=groups
            )
        )
    return jnp.concatenate(returned, axis=0)


def solution(mesh):
    tokens = P(AXES, None)
    return jax.shard_map(
        body,
        mesh=mesh,
        in_specs=(
            tokens,
            tokens,
            tokens,
            tokens,
            P("head", None, None),
            P("head", None, None),
            P("head", None, None),
            P(),
            P(),
        ),
        out_specs=tokens,
        check_vma=False,
    )
```

```python
import functools
import math

import jax
import jax.numpy as jnp
from jax import lax
from jax.experimental import pallas as pl
from jax.experimental.pallas import tpu as pltpu
from jax.sharding import PartitionSpec as P

FDIM = 512
HID = 1024
AHD = 128
WINDOW = 512
NS_ITERS = 3
LEN = 2048
HALF = 128
LOW = 896
HIGH = 1152
SPLIT = 8
BLOCK = LEN // SPLIT

linear_coef = 3.4445
cubic_coef = -4.775
quintic_coef = 2.0315
rms_epsilon = 1e-05
norm_epsilon = 1e-06
MASKED = -1e30
EXP2_SCALE = math.log2(math.e) / math.sqrt(AHD)

AXES = ("tok", "head")
F32 = jnp.float32
BF16 = jnp.bfloat16


CHIPS = 4
KV_ROWS = 528
RATE_ROW = 512
VMEM_LIMIT = 60 * 1024 * 1024


def place_of(block):
    return (block % CHIPS) * 2 + block // CHIPS


class Fetcher:
    def __init__(self, sems):
        self.sems = sems
        self.copies = []

    def __call__(self, src, dst):
        copy = pltpu.make_async_copy(src, dst, self.sems.at[len(self.copies)])
        copy.start()
        self.copies.append(copy)

    def choose(self, options, dst):
        sem = self.sems.at[len(self.copies)]
        for cond, src in options:

            @pl.when(cond)
            def _(src=src):
                pltpu.make_async_copy(src, dst, sem).start()

        self.copies.append(pltpu.make_async_copy(options[0][1], dst, sem))

    def wait(self, first=0, last=None):
        for copy in self.copies[first:last]:
            copy.wait()


def position():
    column = lax.axis_index("head")
    tok = lax.axis_index("tok")
    return column, lax.rem(tok, 2), lax.div(tok, 2)


def pack_kernel(keys, values, queries, rates, *rest):
    kv_outs = rest[: 2 * CHIPS]
    q_out, q_swap = rest[2 * CHIPS : 2 * CHIPS + 2]
    kbuf, vbuf, qbuf, lines, in_sems, sems = rest[2 * CHIPS + 2 :]
    column, parity, _ = position()
    load = Fetcher(in_sems)
    fetch = Fetcher(sems)
    load(keys, kbuf)
    load(values, vbuf)
    load(queries, qbuf)
    turned = rates[...].astype(F32)
    place = lax.broadcasted_iota(jnp.int32, turned.shape, 0)
    targets = []
    for which in range(2):
        core = parity if which == 0 else 1 - parity
        for slot in range(CHIPS):
            head = 2 * lax.rem(column + slot, CHIPS) + core
            targets.append((which * CHIPS + slot, head))
    for index, head in targets:
        line = jnp.sum(jnp.where(place == head, turned, 0.0), axis=0, keepdims=True)
        lines[index, :, pl.ds(0, BLOCK)] = jnp.broadcast_to(line, (16, BLOCK)).astype(BF16)
        lines[index, :, pl.ds(BLOCK, FDIM - BLOCK)] = jnp.zeros((16, FDIM - BLOCK), BF16)
    for index, head in targets:
        fetch(lines.at[index], kv_outs[index].at[pl.ds(RATE_ROW, 16)])
    for part, buf in ((0, kbuf), (1, vbuf), (2, qbuf)):
        load.wait(part, part + 1)
        for index, head in targets:
            cols = pl.ds(pl.multiple_of(head * FDIM, FDIM), FDIM)
            if part < 2:
                dst = kv_outs[index].at[pl.ds(part * BLOCK, BLOCK)]
            else:
                dst = (q_out, q_swap)[index // CHIPS].at[index % CHIPS]
            fetch(buf.at[:, cols], dst)
    fetch.wait()


def pack(keys, values, queries, rates):
    hbm = pl.BlockSpec(memory_space=pltpu.HBM)
    kv_shape = jax.ShapeDtypeStruct((KV_ROWS, FDIM), BF16)
    q_shape = jax.ShapeDtypeStruct((CHIPS, BLOCK, FDIM), BF16)
    width = CHIPS * 2 * FDIM
    outs = pl.pallas_call(
        pack_kernel,
        name="pack",
        out_shape=(kv_shape,) * (2 * CHIPS) + (q_shape, q_shape),
        in_specs=[hbm, hbm, hbm, pl.BlockSpec(memory_space=pltpu.VMEM)],
        out_specs=(hbm,) * (2 * CHIPS + 2),
        scratch_shapes=[
            pltpu.VMEM((BLOCK, width), BF16),
            pltpu.VMEM((BLOCK, width), BF16),
            pltpu.VMEM((BLOCK, width), BF16),
            pltpu.VMEM((2 * CHIPS, 16, FDIM), BF16),
            pltpu.SemaphoreType.DMA((3,)),
            pltpu.SemaphoreType.DMA((32,)),
        ],
        compiler_params=pltpu.CompilerParams(vmem_limit_bytes=VMEM_LIMIT),
        cost_estimate=pl.CostEstimate(flops=0, bytes_accessed=24_000_000, transcendentals=0),
    )(keys, values, queries, rates)
    return outs[:CHIPS], outs[CHIPS : 2 * CHIPS], *outs[2 * CHIPS :]


def dot(a, b):
    return lax.dot_general(a, b, (((1,), (0,)), ((), ())), preferred_element_type=F32)


def dot_nt(a, b):
    return lax.dot_general(a, b, (((1,), (1,)), ((), ())), preferred_element_type=F32)


def update_kernel(
    bounds,
    own0,
    own1,
    own2,
    own3,
    other0,
    other1,
    other2,
    other3,
    gate_hbm,
    up_hbm,
    down_hbm,
    gate_out,
    up_out,
    down_out,
    new_gate,
    new_up,
    new_down,
    kbuf,
    vbuf,
    rbuf,
    wg,
    wu,
    wd,
    wdt,
    hid,
    dgate,
    dup,
    target,
    kt,
    tt,
    grads,
    xs,
    grams,
    sems,
    out_sems,
):
    column, parity, sequence = position()
    bound = bounds[sequence]
    fetch = Fetcher(sems)
    owns = (own0, own1, own2, own3)
    others = (other0, other1, other2, other3)
    core0, core1 = parity == 0, parity == 1

    def low_part(rows, make_dst):
        for slot in range(CHIPS):
            source = lax.rem(column + CHIPS - slot, CHIPS)
            fetch.choose(
                [(core0, owns[slot].at[rows]), (core1, others[slot].at[rows])], make_dst(source)
            )

    def top_part(rows, dst):
        options = []
        for slot in range(CHIPS):
            options.append((core0 & (column == slot), others[slot].at[rows]))
            options.append((core1 & (column == slot), owns[slot].at[rows]))
        fetch.choose(options, dst)

    def rows_at(buf):
        return lambda block: buf.at[pl.ds(pl.multiple_of(block * BLOCK, BLOCK), BLOCK)]

    fetch(down_hbm.at[parity], wd)
    low_part(pl.ds(0, BLOCK), rows_at(kbuf))
    top_part(pl.ds(0, HALF), kbuf.at[pl.ds(CHIPS * BLOCK, HALF)])
    low_part(pl.ds(BLOCK, BLOCK), rows_at(vbuf))
    top_part(pl.ds(BLOCK, HALF), vbuf.at[pl.ds(CHIPS * BLOCK, HALF)])
    low_part(pl.ds(RATE_ROW, 16), lambda block: rbuf.at[block])
    top_part(pl.ds(RATE_ROW, 16), rbuf.at[CHIPS])
    fetch(gate_hbm.at[parity], wg)
    fetch(up_hbm.at[parity], wu)
    fetch.wait(0, 1)
    wdt[...] = wd[...].T
    fetch.wait(1, 6)
    kt[...] = kbuf[...].T
    fetch.wait(6, 16)
    for block in range(CHIPS + 1):
        count = min(BLOCK, HIGH - block * BLOCK)
        rows = pl.ds(block * BLOCK, count)
        rate = rbuf[block].astype(F32)[:8, :count].T[:, :1]
        place = block * BLOCK + lax.broadcasted_iota(jnp.int32, (count, 1), 0)
        weighted = rate * vbuf[rows, :].astype(F32)
        target[rows, :] = jnp.where(place < bound, weighted, 0.0).astype(BF16)
    tt[...] = target[...].T
    fetch.wait(16)
    step = 384
    for part in range(HIGH // step):
        rows = pl.ds(part * step, step)
        k_rows = kbuf[rows, :]
        t_rows = target[rows, :]
        for tile in range(HID // 256):
            cols = pl.ds(tile * 256, 256)
            pre_gate = dot(k_rows, wg[:, cols])
            pre_up = dot(k_rows, wu[:, cols])
            back = dot(t_rows, wdt[:, cols])
            logistic = 1.0 / (1.0 + jnp.exp(-pre_gate))
            act = pre_gate * logistic
            slope = logistic * (1.0 + pre_gate * (1.0 - logistic))
            hid[rows, cols] = (act * pre_up).astype(BF16)
            dgate[rows, cols] = (back * pre_up * slope).astype(BF16)
            dup[rows, cols] = (back * act).astype(BF16)

    for which, (left, right) in enumerate(((kt, dgate), (kt, dup), (tt, hid))):
        total = jnp.zeros((1, 256), F32)
        for tile in range(HID // 256):
            cols = pl.ds(tile * 256, 256)
            grad = dot(left[...], right[:, cols])
            grads[which, :, cols] = grad
            total += jnp.sum(grad * grad, axis=0, keepdims=True)
        inv = 1.0 / jnp.sqrt(jnp.sum(total, axis=1, keepdims=True) + norm_epsilon)
        for tile in range(HID // 256):
            cols = pl.ds(tile * 256, 256)
            xs[which, :, cols] = (grads[which, :, cols] * inv).astype(BF16)

    def iteration(_, carry):
        for which in range(3):
            for top, left in ((0, 0), (0, 1), (1, 1)):
                rows, cols = pl.ds(top * 256, 256), pl.ds(left * 256, 256)
                block = dot_nt(xs[which, rows, :], xs[which, cols, :]).astype(BF16)
                grams[which, rows, cols] = block
                if top != left:
                    grams[which, cols, rows] = block.T
        for which in range(3):
            for top, left in ((0, 0), (0, 1), (1, 1)):
                rows, cols = pl.ds(top * 256, 256), pl.ds(left * 256, 256)
                square = dot(grams[which, rows, :], grams[which, :, cols])
                mixed = cubic_coef * grams[which, rows, cols].astype(F32) + quintic_coef * square
                block = mixed.astype(BF16)
                grams[3 + which, rows, cols] = block
                if top != left:
                    grams[3 + which, cols, rows] = block.T
        for which in range(3):
            mix = grams[3 + which]
            for tile in range(4):
                cols = pl.ds(tile * 256, 256)
                old = xs[which, :, cols]
                xs[which, :, cols] = (linear_coef * old.astype(F32) + dot(mix, old)).astype(BF16)
        return carry

    lax.fori_loop(0, NS_ITERS, iteration, 0, unroll=True)

    stores = Fetcher(out_sems)
    for which, (start, out, target_hbm) in enumerate(
        ((wg, new_gate, gate_out), (wu, new_up, up_out))
    ):
        for tile in range(HID // 256):
            cols = pl.ds(tile * 256, 256)
            wide = start[:, cols].astype(F32)
            moved = wide + xs[which, :, cols].astype(F32)
            aim = jnp.sqrt(jnp.sum(wide * wide, axis=0, keepdims=True) + norm_epsilon)
            actual = jnp.sqrt(jnp.sum(moved * moved, axis=0, keepdims=True) + norm_epsilon)
            out[:, cols] = (moved * (aim / actual)).astype(BF16)
        stores(out, target_hbm)
    for tile in range(FDIM // 128):
        rows = pl.ds(tile * 128, 128)
        wide = wdt[rows, :].astype(F32)
        moved = wide + xs[2, rows, :].astype(F32)
        aim = jnp.sqrt(jnp.sum(wide * wide, axis=1, keepdims=True) + norm_epsilon)
        actual = jnp.sqrt(jnp.sum(moved * moved, axis=1, keepdims=True) + norm_epsilon)
        new_down[rows, :] = (moved * (aim / actual)).astype(BF16)
    stores(new_down, down_out)
    stores.wait()


def fast_update(bounds, owns, others, starts):
    hbm = pl.BlockSpec(memory_space=pltpu.HBM)
    return pl.pallas_call(
        update_kernel,
        name="fast_update",
        out_shape=(
            jax.ShapeDtypeStruct((FDIM, HID), BF16),
            jax.ShapeDtypeStruct((FDIM, HID), BF16),
            jax.ShapeDtypeStruct((FDIM, HID), BF16),
        ),
        in_specs=[pl.BlockSpec(memory_space=pltpu.SMEM)] + [hbm] * 11,
        out_specs=(hbm, hbm, hbm),
        scratch_shapes=[
            pltpu.VMEM((FDIM, HID), BF16),
            pltpu.VMEM((FDIM, HID), BF16),
            pltpu.VMEM((FDIM, HID), BF16),
            pltpu.VMEM((HIGH, FDIM), BF16),
            pltpu.VMEM((HIGH, FDIM), BF16),
            pltpu.VMEM((CHIPS + 1, 16, FDIM), BF16),
            pltpu.VMEM((FDIM, HID), BF16),
            pltpu.VMEM((FDIM, HID), BF16),
            pltpu.VMEM((HID, FDIM), BF16),
            pltpu.VMEM((FDIM, HID), BF16),
            pltpu.VMEM((HIGH, HID), BF16),
            pltpu.VMEM((HIGH, HID), BF16),
            pltpu.VMEM((HIGH, HID), BF16),
            pltpu.VMEM((HIGH, FDIM), BF16),
            pltpu.VMEM((FDIM, HIGH), BF16),
            pltpu.VMEM((FDIM, HIGH), BF16),
            pltpu.VMEM((3, FDIM, HID), F32),
            pltpu.VMEM((3, FDIM, HID), BF16),
            pltpu.VMEM((6, FDIM, FDIM), BF16),
            pltpu.SemaphoreType.DMA((18,)),
            pltpu.SemaphoreType.DMA((3,)),
        ],
        compiler_params=pltpu.CompilerParams(vmem_limit_bytes=VMEM_LIMIT),
        cost_estimate=pl.CostEstimate(
            flops=20_000_000_000, bytes_accessed=12_000_000, transcendentals=1_200_000
        ),
    )(bounds, *owns, *others, *starts)


def apply_kernel(
    chunk,
    bounds,
    own_q,
    other_q,
    q1,
    q2,
    q3,
    own0,
    own1,
    own2,
    own3,
    other0,
    other1,
    other2,
    other3,
    halo,
    gate_hbm,
    up_hbm,
    down_hbm,
    gate_new,
    up_new,
    down_new,
    gain_hbm,
    out_hbm,
    out,
    qc,
    kbuf,
    vbuf,
    wg,
    wu,
    wd,
    new_gate,
    new_up,
    new_down,
    gain,
    hid,
    raw,
    before,
    fast,
    sems,
    out_sem,
    scores,
    rounded,
):
    column, parity, sequence = position()
    bound = bounds[sequence]
    owned = 2 * column + parity
    fetch = Fetcher(sems)

    def q_rows_of(core, source):
        return qc.at[pl.ds(pl.multiple_of((core * CHIPS + source) * HALF, HALF), HALF)]

    def sender(slot):
        return lax.rem(column + CHIPS - slot, CHIPS)

    fetch(gate_hbm.at[parity], wg)
    fetch(up_hbm.at[parity], wu)
    q_src = pl.ds(chunk * HALF, HALF)
    fetch(own_q.at[0, q_src], q_rows_of(parity, column))
    fetch(other_q.at[0, q_src], q_rows_of(1 - parity, column))
    for slot, array in ((1, q1), (2, q2), (3, q3)):
        fetch(array.at[q_src], q_rows_of(parity, sender(slot)))
        fetch(array.at[pl.ds(BLOCK + chunk * HALF, HALF)], q_rows_of(1 - parity, sender(slot)))
    early = len(fetch.copies)
    fetch(down_hbm.at[parity], wd)
    downs = len(fetch.copies)
    fetch(gate_new, new_gate)
    fetch(up_new, new_up)
    fetch(down_new, new_down)
    fetch(gain_hbm, gain)
    first = len(fetch.copies)
    fetch.wait(0, early)
    for which, buf in ((0, kbuf), (1, vbuf)):
        rows = pl.ds(which * BLOCK, BLOCK)

        def rows_at(core, source, buf=buf):
            start = WINDOW + (core * CHIPS + source) * BLOCK
            return buf.at[pl.ds(pl.multiple_of(start, BLOCK), BLOCK)]

        fetch(halo.at[pl.ds(which * WINDOW, WINDOW)], buf.at[pl.ds(0, WINDOW)])
        for slot, own, other in (
            (0, own0, other0),
            (1, own1, other1),
            (2, own2, other2),
            (3, own3, other3),
        ):
            fetch(own.at[rows], rows_at(parity, sender(slot)))
            fetch(other.at[rows], rows_at(1 - parity, sender(slot)))

    def swiglu(rows, gate, up, down, product, store, ready):
        in_rows = qc[rows, :]
        for tile in range(HID // 256):
            cols = pl.ds(tile * 256, 256)
            pre_gate = dot(in_rows, gate[:, cols])
            pre_up = dot(in_rows, up[:, cols])
            hid[pl.ds(0, rows.size), cols] = (
                pre_gate / (1.0 + jnp.exp(-pre_gate)) * pre_up
            ).astype(BF16)
        ready()
        store(product(hid[pl.ds(0, rows.size), :], down[...]))

    edge = 4 if chunk == 0 else 3
    old_rows = pl.ds(0, (edge + 1) * HALF)
    new_rows = pl.ds(edge * HALF, (SPLIT - edge) * HALF)

    def store_old(value):
        raw[pl.ds(0, edge * HALF), :] = value[: edge * HALF]
        before[...] = value[edge * HALF :]

    def store_new(value):
        raw[new_rows, :] = value

    swiglu(old_rows, wg, wu, wd, dot, store_old, lambda: fetch.wait(early, downs))
    fetch.wait(downs, first)
    swiglu(new_rows, new_gate, new_up, new_down, dot_nt, store_new, lambda: None)
    mid = pl.ds(edge * HALF, HALF)
    place = edge * BLOCK + chunk * HALF + lax.broadcasted_iota(jnp.int32, (HALF, 1), 0)
    raw[mid, :] = jnp.where(place < bound, before[...], raw[mid, :])
    gain_row = gain[pl.ds(owned, 1), :]
    for block in range(SPLIT):
        rows = pl.ds(block * HALF, HALF)
        value = raw[rows, :]
        root = jnp.sqrt(jnp.mean(value * value, axis=1, keepdims=True) + rms_epsilon)
        fast[rows, :] = (value / root * gain_row).astype(BF16)
    fetch.wait(first)

    row_iota = lax.broadcasted_iota(jnp.int32, (HALF, HALF), 0)
    col_iota = lax.broadcasted_iota(jnp.int32, (HALF, HALF), 1)
    keep_old = col_iota > row_iota
    keep_own = col_iota <= row_iota

    def attend(block, edge_block):
        base = pl.multiple_of(block * BLOCK + chunk * HALF, HALF)
        q_rows = pl.ds(pl.multiple_of(block * HALF, HALF), HALF)
        o_rows = pl.ds(pl.multiple_of(place_of(block) * HALF, HALF), HALF)
        keys = pl.ds(base, WINDOW + HALF)
        heads = range(FDIM // AHD)
        for head in heads:
            cols = pl.ds(head * AHD, AHD)
            scores[head] = dot_nt(qc[q_rows, cols], kbuf[keys, cols])
        totals = []
        for head in heads:
            parts = [scores[head, :, i * HALF : (i + 1) * HALF] for i in range(5)]
            parts[0] = jnp.where(keep_old, parts[0], MASKED)
            parts[4] = jnp.where(keep_own, parts[4], MASKED)
            if edge_block:
                for i in range(4):
                    absent = (sequence == 0) & (base + i * HALF < WINDOW)
                    parts[i] = jnp.where(absent, MASKED, parts[i])
            top = jnp.max(functools.reduce(jnp.maximum, parts), axis=1, keepdims=True)
            total = None
            for i in range(5):
                weight = jnp.exp2((parts[i] - top) * EXP2_SCALE)
                rounded[head, :, i * HALF : (i + 1) * HALF] = weight.astype(BF16)
                total = weight if total is None else total + weight
            totals.append(jnp.sum(total, axis=1, keepdims=True))
        for head in heads:
            cols = pl.ds(head * AHD, AHD)
            mixed = dot(rounded[head], vbuf[keys, cols])
            attn = (mixed / totals[head]).astype(BF16)
            out[o_rows, cols] = (attn.astype(F32) + fast[q_rows, cols].astype(F32)).astype(BF16)

    def edge_body(block, carry):
        attend(block, True)
        return carry

    def main_body(block, carry):
        attend(block, False)
        return carry

    lax.fori_loop(0, 2, edge_body, 0, unroll=2)
    lax.fori_loop(2, SPLIT, main_body, 0, unroll=2)
    copy = pltpu.make_async_copy(out, out_hbm, out_sem)
    copy.start()
    copy.wait()


def apply_chunk(chunk, bounds, local_q, q_parts, owns, others, halo, starts, news, gain):
    hbm = pl.BlockSpec(memory_space=pltpu.HBM)
    rows = SPLIT * HALF
    return pl.pallas_call(
        functools.partial(apply_kernel, chunk),
        name="apply_attend",
        out_shape=jax.ShapeDtypeStruct((rows, FDIM), BF16),
        in_specs=[pl.BlockSpec(memory_space=pltpu.SMEM)] + [hbm] * 21,
        out_specs=hbm,
        scratch_shapes=[
            pltpu.VMEM((rows, FDIM), BF16),
            pltpu.VMEM((rows, FDIM), BF16),
            pltpu.VMEM((WINDOW + LEN, FDIM), BF16),
            pltpu.VMEM((WINDOW + LEN, FDIM), BF16),
            pltpu.VMEM((FDIM, HID), BF16),
            pltpu.VMEM((FDIM, HID), BF16),
            pltpu.VMEM((HID, FDIM), BF16),
            pltpu.VMEM((FDIM, HID), BF16),
            pltpu.VMEM((FDIM, HID), BF16),
            pltpu.VMEM((FDIM, HID), BF16),
            pltpu.VMEM((SPLIT, FDIM), F32),
            pltpu.VMEM((5 * HALF, HID), BF16),
            pltpu.VMEM((rows, FDIM), F32),
            pltpu.VMEM((HALF, FDIM), F32),
            pltpu.VMEM((rows, FDIM), BF16),
            pltpu.SemaphoreType.DMA((33,)),
            pltpu.SemaphoreType.DMA,
            pltpu.VMEM((FDIM // AHD, HALF, WINDOW + HALF), F32),
            pltpu.VMEM((FDIM // AHD, HALF, WINDOW + HALF), BF16),
        ],
        compiler_params=pltpu.CompilerParams(vmem_limit_bytes=VMEM_LIMIT),
        cost_estimate=pl.CostEstimate(
            flops=8_000_000_000, bytes_accessed=14_000_000, transcendentals=4_000_000
        ),
    )(bounds, *local_q, *q_parts, *owns, *others, halo, *starts, *news, gain)


def body(queries, keys, values, token_rates, gate_start, up_start, down_start, norm_gain, bounds):
    shards = lax.axis_size("tok") * lax.axis_size("head")
    column = lax.axis_index("head")
    parity = lax.axis_index("tok") % 2
    groups = [
        [s * SPLIT + place for place in sorted(range(SPLIT), key=lambda b: (b % CHIPS, b // CHIPS))]
        for s in range(shards // SPLIT)
    ]
    tok_count = lax.axis_size("tok")

    def along(array, slot):
        return lax.ppermute(array, "head", [(i, (i + slot) % CHIPS) for i in range(CHIPS)])

    def across(array, slot):
        pairs = [
            (t * CHIPS + i, (t ^ 1) * CHIPS + (i + slot) % CHIPS)
            for t in range(tok_count)
            for i in range(CHIPS)
        ]
        return lax.ppermute(array, AXES, pairs)

    def next_segment(array):
        return lax.ppermute(array, "tok", [(i, i + 2) for i in range(tok_count - 2)])

    order = (1, 3, 2)
    own_kv, swap_kv, own_q, swap_q = pack(keys, values, queries, token_rates.T)
    owns, others = [own_kv[0]] * CHIPS, [None] * CHIPS
    for slot in order:
        owns[slot] = along(own_kv[slot], slot)
    for slot in order + (0,):
        others[slot] = across(swap_kv[slot], slot)
    other_q = across(swap_q, 0)
    q_parts = [None] * CHIPS
    for slot in order:
        part = jnp.concatenate([own_q[slot], other_q[slot]], axis=0)
        others[slot], part = lax.optimization_barrier((others[slot], part))
        q_parts[slot] = along(part, slot)

    first_core = parity == 0

    def tail(source):
        value = jnp.where(first_core, others[0], owns[0])
        for slot in order:
            here = jnp.where(first_core, others[slot], owns[slot])
            value = jnp.where(column == (source + slot) % CHIPS, here, value)
        return value

    tails = [tail(source) for source in (2, 3)]
    halo = next_segment(
        jnp.concatenate(
            [t[part * BLOCK : (part + 1) * BLOCK] for part in range(2) for t in tails], axis=0
        )
    )

    starts = (gate_start, up_start, down_start)
    news = fast_update(bounds, owns, others, starts)
    gain = norm_gain.reshape(-1, FDIM)
    returned = []
    for chunk in range(2):
        out = apply_chunk(
            chunk,
            bounds,
            (own_q, other_q),
            q_parts[1:],
            owns,
            others,
            halo,
            starts,
            news,
            gain,
        )
        returned.append(
            lax.all_to_all(
                out, AXES, split_axis=0, concat_axis=1, tiled=True, axis_index_groups=groups
            )
        )
    return jnp.concatenate(returned, axis=0)


def solution(mesh):
    tokens = P(AXES, None)
    return jax.shard_map(
        body,
        mesh=mesh,
        in_specs=(
            tokens,
            tokens,
            tokens,
            tokens,
            P("head", None, None),
            P("head", None, None),
            P("head", None, None),
            P(),
            P(),
        ),
        out_specs=tokens,
        check_vma=False,
    )
```
